256 devices in a mesh: gene: 4 (over z_hi), cell: 64 (over x, y, z_lo, core).
Axes of the slice: x: 4, y: 4, z: 8 (z_hi: 4, z_lo: 2; z = z_hi * 2 + z_lo), core: 2. Of those that a mesh axis runs over, the one named last changes fastest.
Arguments:
- counts: int32 [16384, 32768], P('gene', 'cell'), may hold values from 0 to 2047, as said below
- w1: bfloat16 [16384, 512], P(('gene', 'cell')), may hold values from 0.099609375 to 2
- h1: float32 [512, 32768], P(None, 'cell'), may hold values from 0.1 to 2
- w2: float32 [512, 64], replicated, may hold values from 0.1 to 2
- h2: float32 [64, 32768], P(None, 'cell'), may hold values from 0.005 to 0.1
Outputs:
- w1_new: bfloat16 [16384, 512], P(('gene', 'cell'))
- h1_new: float32 [512, 32768], P(None, 'cell')
- w2_new: float32 [512, 64], replicated
- h2_new: float32 [64, 32768], P(None, 'cell')
The draws below stay inside these ranges and needn't reach their ends.
Inputs may be any that keep to these rules, and one draw needn't show every extreme that they name: `counts`: counts are whole numbers; a gene's and a cell's typical depth vary, and cells later in the order run deeper.
All inputs are finite; a program needn't handle non-finite values.
Results may differ from the reference program's by a relative error of at most 0.0013.
The reference program's roundings to bfloat16 on the way count: a program that leaves them out, or rounds other values in their place, can miss the bound.
Values may be sent and summed in bfloat16 or wider, within the bound.
A program may use at most 64 MiB of HBM per device.

```python
import math
import jax
import jax.numpy as jnp
from jax import lax

G = 16384
K1 = 512
K2 = 64
C = 32768


def draw_counts(key, part):
    key_cell = jax.random.fold_in(key, 11)
    key_gene = jax.random.fold_in(key, 12)
    key_value = jax.random.fold_in(key, 13)
    column = jnp.arange(C, dtype=jnp.int32)
    depth_top = 16 + 48 * (column + 1) // C
    cell_level = jax.random.randint(key_cell, (C,), 1, depth_top + 1)
    gene_level = jax.random.randint(key_gene, (G,), 1, 9)
    ceiling = 4 * gene_level[:, None] * cell_level[None, :] - 1
    return jax.random.randint(key_value, (G, C), 0, ceiling + 1)


def block_scale(own_key, extent, cuts, smallest, largest):
    gain, own = 1.0, jax.random.fold_in(own_key, 6)
    for axis_at, parts in cuts:
        steps = jnp.exp(jax.random.uniform(jax.random.fold_in(own, axis_at), (parts,), jnp.float32, smallest / len(cuts), largest / len(cuts)))
        gain = gain * jnp.repeat(steps, extent[axis_at] // parts).reshape([-1 if axis == axis_at else 1 for axis in range(len(extent))])
    return gain


def setup_inputs(seed: int = 0) -> dict:
    streams_of = jax.random.split(jax.random.key(seed), 6)
    counts = draw_counts(jax.random.fold_in(streams_of[5], 71), 0)
    w1 = jnp.clip(jnp.exp(math.log(2.0) - 2.9996462 * jax.random.uniform(streams_of[1], (G, K1), jnp.float32) ** block_scale(streams_of[1], (G, K1), ((0, 256),), -0.2, 0.2)), 0.099609375, 2.0).astype(jnp.bfloat16)
    h1 = jnp.clip(jnp.exp(math.log(2.0) - 2.9957323 * jax.random.uniform(streams_of[2], (K1, C), jnp.float32) ** block_scale(streams_of[2], (K1, C), ((1, 64),), -0.2, 0.2)), 0.1, 2.0)
    w2 = jnp.clip(jnp.exp(jax.random.uniform(streams_of[3], (K1, K2), jnp.float32, math.log(0.1), math.log(2.0))), 0.1, 2.0)
    h2 = jnp.clip(jnp.exp(math.log(0.1) - 2.9957323 * jax.random.uniform(streams_of[4], (K2, C), jnp.float32) ** block_scale(streams_of[4], (K2, C), ((1, 64),), -0.2, 0.2)), 0.005, 0.1)
    return {"counts": counts, "w1": w1, "h1": h1, "w2": w2, "h2": h2}


def reference(counts, w1, h1, w2, h2):
    hi = lax.Precision.HIGHEST
    block = 512
    nblocks = G // block
    w1_blocks = w1.reshape(nblocks, block, K1)
    v_blocks = counts.reshape(nblocks, block, C)
    h1_low = h1.astype(jnp.bfloat16)
    colsum = jnp.sum(w1.astype(jnp.float32), axis=0)

    def first(acc, pair):
        wb, vb = pair
        approx = jnp.dot(wb, h1_low, preferred_element_type=jnp.float32)
        ratio = (vb.astype(jnp.float32) / approx).astype(jnp.bfloat16)
        return acc + jnp.dot(wb.T, ratio, preferred_element_type=jnp.float32), None

    h1_num, unused = lax.scan(first, jnp.zeros((K1, C), jnp.float32), (w1_blocks, v_blocks))
    h1_new = h1 * h1_num / colsum[:, None]
    h1_low2 = h1_new.astype(jnp.bfloat16)

    def second(pair):
        wb, vb = pair
        approx = jnp.dot(wb, h1_low2, preferred_element_type=jnp.float32)
        ratio = (vb.astype(jnp.float32) / approx).astype(jnp.bfloat16)
        return jnp.dot(ratio, h1_low2.T, preferred_element_type=jnp.float32)

    w1_num = lax.map(second, (w1_blocks, v_blocks)).reshape(G, K1)
    rowsum = jnp.sum(h1_new, axis=1)
    w1_new = (w1.astype(jnp.float32) * w1_num / rowsum[None, :]).astype(jnp.bfloat16)

    ratio3 = h1_new / jnp.dot(w2, h2, precision=hi)
    h2_new = h2 * jnp.dot(w2.T, ratio3, precision=hi) / jnp.sum(w2, axis=0)[:, None]
    ratio4 = h1_new / jnp.dot(w2, h2_new, precision=hi)
    w2_num = jnp.dot(ratio4, h2_new.T, precision=hi)
    w2_new = w2 * w2_num / jnp.sum(h2_new, axis=1)[None, :]
    return w1_new, h1_new, w2_new, h2_new
```

```python
import functools

import jax
import jax.numpy as jnp
from jax import lax
from jax.experimental import pallas as pl
from jax.experimental.pallas import tpu as pltpu
from jax.sharding import PartitionSpec as P

NX, NY, NZ, NC = 4, 4, 2, 2
NG = 4
F32, BF16 = jnp.float32, jnp.bfloat16
HI = lax.Precision.HIGHEST

S_Z = 0
S_A2 = 1
S_A3 = S_A2 + 6
S_F = S_A3 + 6
S_CS = S_F + 8
S_N = S_CS + 3
S_HB = S_N + 3
S_E1 = S_HB + 6
S_X1 = S_E1 + 8
S_X2 = S_X1 + 6
S_ZZ = S_X2 + 6
S_SC = S_ZZ + 1
S_SZ = S_SC + 1
S_SX = S_SZ + 1
S_SY = S_SX + 3
S_SG = S_SY + 3
S_ALL = S_SG + 3


def nt(a, b, precision=None):
    return lax.dot_general(
        a, b, (((1,), (1,)), ((), ())), preferred_element_type=F32, precision=precision
    )


def kernel(
    counts,
    w1,
    h1,
    w2,
    h2,
    w1_out,
    h1_out,
    w2_out,
    h2_out,
    wg,
    cnt,
    hl,
    num,
    nrecv,
    cs,
    csr,
    hbuf,
    e1s,
    e1r,
    part,
    xr,
    xr2,
    fin,
    zr,
    sm,
    smc,
    smz,
    smx,
    smy,
    smg,
    snd,
    rcv,
    csem,
):
    g = lax.axis_index("gene")
    ci = lax.axis_index("cell")
    mx, my, mz, mc = ci // 16, (ci // 4) % 4, (ci // 2) % 2, ci % 2
    oz, oc = 1 - mz, 1 - mc

    def cell(x, y, z, c):
        return ((x * NY + y) * NZ + z) * NC + c

    def at_x(d):
        return (mx + d) % NX

    def at_y(d):
        return (my + d) % NY

    def at_g(d):
        return (g + d) % NG

    def copy(src, dst, sem, gene, to):
        return pltpu.make_async_remote_copy(
            src_ref=src,
            dst_ref=dst,
            send_sem=snd.at[sem],
            recv_sem=rcv.at[sem],
            device_id=(gene, to),
            device_id_type=pl.DeviceIdType.MESH,
        )

    sibling = cell(mx, my, mz, oc)
    z_pair = cell(mx, my, oz, mc)
    x_cell = lambda d: cell(at_x(d), my, mz, mc)
    y_cell = lambda d: cell(mx, at_y(d), mz, mc)

    read_counts = pltpu.make_async_copy(counts, cnt, csem.at[0])
    read_counts.start()

    barrier = pltpu.get_barrier_semaphore()
    partners = [(g, sibling), (g, z_pair)]
    for d in range(1, 4):
        partners += [(g, x_cell(d)), (g, y_cell(d)), (at_g(d), ci)]
    for gene, to in partners:
        pl.semaphore_signal(
            barrier, inc=1, device_id=(gene, to), device_id_type=pl.DeviceIdType.MESH
        )

    wg[mx, my, mz, mc] = w1[...]
    hl[...] = h1[...].astype(BF16)
    num[...] = jnp.zeros_like(num)
    cs[...] = jnp.zeros_like(cs)
    pl.semaphore_wait(barrier, len(partners))

    own = wg.at[mx, my, mz, mc]
    go_z = copy(own, own, S_Z, g, z_pair)
    go_z.start()
    go_z.wait_recv()

    def stage_two(h, d):
        src = wg.at[mx, my, :, mc, h]
        return copy(src, src, S_A2 + 3 * h + d - 1, g, x_cell(d) if h == 0 else y_cell(d))

    for d in (1, 3, 2):
        for h in range(2):
            stage_two(h, d).start()
    for d in (1, 3, 2):
        for h in range(2):
            stage_two(h, d).wait_recv()

    def column(h, d):
        return wg.at[:, at_y(4 - d), :, mc, 0] if h == 0 else wg.at[at_x(4 - d), :, :, mc, 1]

    def stage_three(h, d):
        src = column(h, 0)
        return copy(src, src, S_A3 + 3 * h + d - 1, g, y_cell(d) if h == 0 else x_cell(d))

    def forward(h, d):
        src = column(h, d)
        return copy(src, src, S_F + 4 * h + d, g, sibling)

    for d in (1, 3, 2):
        for h in range(2):
            stage_three(h, d).start()
    for h in range(2):
        forward(h, 0).start()

    read_counts.wait()

    def pass_on(d):
        for h in range(2):
            stage_three(h, d).wait_recv()
            forward(h, d).start()

    def first(w, v):
        approx = jnp.dot(w, hl[...], preferred_element_type=F32)
        ratio = (v.astype(F32) / approx).astype(BF16)
        add = lax.dot_general(
            w, ratio, (((0,), (0,)), ((), ())), preferred_element_type=F32
        )
        for j in range(NG):
            num[j] += add[:, j * 128 : (j + 1) * 128]
        cs[...] += jnp.sum(w.astype(F32).reshape(-1, 8, w.shape[1]), axis=0)

    def first_step(t, carry):
        d = t + t // 2 - 2 * (t // 3)
        forward(0, d).wait_recv()
        first(
            wg[:, at_y(4 - d), :, :, 0].reshape(512, 512),
            cnt[:, at_y(4 - d), :, :, 0].reshape(512, 512),
        )
        forward(1, d).wait_recv()
        first(
            wg[at_x(4 - d), :, :, :, 1].reshape(512, 512),
            cnt[at_x(4 - d), :, :, :, 1].reshape(512, 512),
        )

        @pl.when(t == 0)
        def _():
            pass_on(1)
            pass_on(3)

        @pl.when(t == 1)
        def _():
            pass_on(2)

        return carry

    lax.fori_loop(0, 4, first_step, 0)

    def send_num(d):
        return copy(num.at[at_g(d)], nrecv.at[d - 1], S_N + d - 1, at_g(d), ci)

    def send_cs(d):
        return copy(cs, csr.at[d - 1], S_CS + d - 1, at_g(d), ci)

    for d in (1, 3, 2):
        send_cs(d).start()
        send_num(d).start()
    for d in (1, 3, 2):
        send_cs(d).wait_recv()
    total = jnp.sum(cs[...] + csr[0] + csr[1] + csr[2], axis=0, keepdims=True)
    colsum = jnp.transpose(jnp.broadcast_to(total, (128, 512)))
    for d in (1, 3, 2):
        send_num(d).wait_recv()
    h1_mine = h1[:, pl.ds(pl.multiple_of(g * 128, 128), 128)]
    fresh = h1_mine * (num[g] + nrecv[0] + nrecv[1] + nrecv[2]) / colsum
    high = fresh.astype(BF16)
    hbuf[0, g] = high
    hbuf[1, g] = (fresh - high.astype(F32)).astype(BF16)

    def send_h(h, d):
        src = hbuf.at[h, g]
        return copy(src, src, S_HB + 3 * h + d - 1, at_g(d), ci)

    for h in range(2):
        for d in (1, 3, 2):
            send_h(h, d).start()
    for d in (1, 3, 2):
        send_h(0, d).wait_recv()
    for j in range(NG):
        hl[:, j * 128 : (j + 1) * 128] = hbuf[0, j]

    def second(w, v):
        approx = jnp.dot(w, hl[...], preferred_element_type=F32)
        ratio = (v.astype(F32) / approx).astype(BF16)
        return nt(ratio, hl[...]).reshape(4, 2, 32, 512)

    def pick(ref, h, i, c):
        d = i + 1
        found = ref[at_x(d), :, :, c, 0] if h == 0 else ref[:, at_y(d), :, c, 1]
        return found.reshape(256, 512)

    def to_sibling(h, i):
        return copy(e1s.at[h, i], e1r.at[h, i], S_E1 + 4 * h + i, g, sibling)

    def along(h, i):
        to = x_cell(i + 1) if h == 0 else y_cell(i + 1)
        return copy(part.at[h, i], xr.at[h, i], S_X1 + 3 * h + i, g, to)

    def second_step(i, carry):
        for h in range(2):
            e1s[h, i] = second(pick(wg, h, i, oc), pick(cnt, h, i, oc))
            to_sibling(h, i).start()
        for h in range(2):
            part[h, i] = second(pick(wg, h, i, mc), pick(cnt, h, i, mc))
        for h in range(2):
            to_sibling(h, i).wait_recv()
            part[h, i] += e1r[h, i]

            @pl.when(i < 3)
            def _():
                along(h, i).start()

        return carry

    lax.fori_loop(0, 4, second_step, 0)

    for d in (1, 3, 2):
        send_h(1, d).wait_recv()
    for j in range(NG):
        h1_out[:, j * 128 : (j + 1) * 128] = hbuf[0, j].astype(F32) + hbuf[1, j].astype(F32)
    w2_t = jnp.transpose(w2[...])
    h1_new = h1_out[...]
    ratio3 = h1_new / jnp.dot(w2[...], h2[...], precision=HI, preferred_element_type=F32)
    lift = jnp.dot(w2_t, ratio3, precision=HI, preferred_element_type=F32)
    h2_out[...] = h2[...] * lift / jnp.sum(w2_t, axis=1, keepdims=True)
    ratio4 = h1_new / jnp.dot(w2[...], h2_out[...], precision=HI, preferred_element_type=F32)
    h2_mine = h2_out[pl.ds(pl.multiple_of(g * 16, 16), 16), :]
    sm[0:16, 0:512] = nt(h2_mine, ratio4, HI)
    sm[0:16, 512:640] = jnp.broadcast_to(jnp.sum(h2_mine, axis=1, keepdims=True), (16, 128))
    sm[16:24, 0:512] = nt(jnp.ones((8, 512), F32), h1_new, HI)
    sm[16:24, 512:640] = jnp.zeros((8, 128), F32)

    sm_c = copy(sm, smc.at[1], S_SC, g, sibling)
    sm_z = copy(smc.at[0], smz, S_SZ, g, z_pair)
    sm_x = lambda d: copy(smx.at[mx], smx.at[mx], S_SX + d - 1, g, x_cell(d))
    sm_y = lambda d: copy(smy.at[my], smy.at[my], S_SY + d - 1, g, y_cell(d))
    sm_g = lambda d: copy(smg.at[g], smg.at[g], S_SG + d - 1, at_g(d), ci)

    def across(h, d):
        src = part.at[h, 3, at_y(d)] if h == 0 else part.at[h, 3, at_x(d)]
        to = y_cell(d) if h == 0 else x_cell(d)
        return copy(src, xr2.at[h, d - 1], S_X2 + 3 * h + d - 1, g, to)

    sm_c.start()
    for h in range(2):
        for i in (0, 2, 1):
            along(h, i).wait_recv()
        part[h, 3] += xr[h, 0] + xr[h, 1] + xr[h, 2]
        for d in (1, 3, 2):
            across(h, d).start()
    sm_c.wait_recv()
    smc[0] = sm[...] + smc[1]
    sm_z.start()
    sm_z.wait_recv()
    smx[mx] = smc[0] + smz[...]
    for d in (1, 3, 2):
        sm_x(d).start()
    for h in range(2):
        for d in (1, 3, 2):
            across(h, d).wait_recv()
    fin[:, 0] = part[0, 3, my] + xr2[0, 0] + xr2[0, 1] + xr2[0, 2]
    fin[:, 1] = part[1, 3, mx] + xr2[1, 0] + xr2[1, 1] + xr2[1, 2]
    last = copy(fin.at[oz], zr, S_ZZ, g, z_pair)
    last.start()
    for d in (1, 3, 2):
        sm_x(d).wait_recv()
    smy[my] = smx[0] + smx[1] + smx[2] + smx[3]
    for d in (1, 3, 2):
        sm_y(d).start()
    for d in (1, 3, 2):
        sm_y(d).wait_recv()
    done = smy[0] + smy[1] + smy[2] + smy[3]
    smg[g] = done[0:16]
    for d in (1, 3, 2):
        sm_g(d).start()
    last.wait_recv()
    w1_num = (fin[mz] + zr[...]).reshape(64, 512)
    rowsum = done[16:17, 0:512]
    w1_now = w1[...].astype(F32).reshape(64, 512)
    w1_out[...] = (w1_now * w1_num / rowsum).astype(BF16)
    for d in (1, 3, 2):
        sm_g(d).wait_recv()
    whole = smg[...].reshape(64, 640)
    w2_out[...] = jnp.transpose(w2_t * whole[:, 0:512] / whole[:, 512:513])

    go_z.wait_send()
    sm_c.wait_send()
    sm_z.wait_send()
    last.wait_send()
    for d in range(1, 4):
        for h in range(2):
            stage_two(h, d).wait_send()
            stage_three(h, d).wait_send()
            send_h(h, d).wait_send()
            along(h, d - 1).wait_send()
            across(h, d).wait_send()
        for sent in (send_num, send_cs, sm_x, sm_y, sm_g):
            sent(d).wait_send()
    for h in range(2):
        for d in range(4):
            forward(h, d).wait_send()
            to_sibling(h, d).wait_send()


def on_device(counts, w1, h1, w2, h2):
    vmem = pl.BlockSpec(memory_space=pltpu.VMEM)
    shape = (NX, NY, NZ, NC, 2, 32, 512)
    return pl.pallas_call(
        kernel,
        out_shape=(
            jax.ShapeDtypeStruct((64, 512), BF16),
            jax.ShapeDtypeStruct((512, 512), F32),
            jax.ShapeDtypeStruct((512, 64), F32),
            jax.ShapeDtypeStruct((64, 512), F32),
        ),
        in_specs=[pl.BlockSpec(memory_space=pl.ANY)] + [vmem] * 4,
        out_specs=(vmem,) * 4,
        scratch_shapes=[
            pltpu.VMEM(shape, BF16),
            pltpu.VMEM(shape, jnp.int32),
            pltpu.VMEM((512, 512), BF16),
            pltpu.VMEM((NG, 512, 128), F32),
            pltpu.VMEM((3, 512, 128), F32),
            pltpu.VMEM((8, 512), F32),
            pltpu.VMEM((3, 8, 512), F32),
            pltpu.VMEM((2, NG, 512, 128), BF16),
            pltpu.VMEM((2, 4, 4, 2, 32, 512), F32),
            pltpu.VMEM((2, 4, 4, 2, 32, 512), F32),
            pltpu.VMEM((2, 4, 4, 2, 32, 512), F32),
            pltpu.VMEM((2, 3, 4, 2, 32, 512), F32),
            pltpu.VMEM((2, 3, 2, 32, 512), F32),
            pltpu.VMEM((2, 2, 32, 512), F32),
            pltpu.VMEM((2, 32, 512), F32),
            pltpu.VMEM((24, 640), F32),
            pltpu.VMEM((2, 24, 640), F32),
            pltpu.VMEM((24, 640), F32),
            pltpu.VMEM((4, 24, 640), F32),
            pltpu.VMEM((4, 24, 640), F32),
            pltpu.VMEM((NG, 16, 640), F32),
            pltpu.SemaphoreType.DMA((S_ALL,)),
            pltpu.SemaphoreType.DMA((S_ALL,)),
            pltpu.SemaphoreType.DMA((1,)),
        ],
        compiler_params=pltpu.CompilerParams(
            collective_id=0, has_side_effects=True, vmem_limit_bytes=60 * 1024 * 1024
        ),
    )(counts.reshape(shape), w1.reshape(2, 32, 512), h1, w2, h2)


def solution(mesh):
    placed = (P("gene", "cell"), P(("gene", "cell"), None), P(None, "cell"), P(), P(None, "cell"))
    return jax.shard_map(
        on_device,
        mesh=mesh,
        in_specs=placed,
        out_specs=(P(("gene", "cell"), None), P(None, "cell"), P(), P(None, "cell")),
        check_vma=False,
    )
```

```python
import jax
import jax.numpy as jnp
from jax import lax
from jax.experimental import pallas as pl
from jax.experimental.pallas import tpu as pltpu
from jax.sharding import PartitionSpec as P

NX, NY, NZ, NC = 4, 4, 2, 2
NG = 4
F32, BF16, I16 = jnp.float32, jnp.bfloat16, jnp.int16
HI = lax.Precision.HIGHEST
TOP = 32767.0
ORDER = (1, 3, 2)

SIZES = dict(
    z=1, a2=6, a3=6, f=8, m=3, n=3, hb=6, h2=3, e1=8, p=6, ps=6, q=6, qs=6, l=1, ls=1,
    s0=3, s1=1, s2=1, s3=3, s4=3, s5=3, s6=1,
)
PLACE, S_ALL = {}, 0
for _name, _size in SIZES.items():
    PLACE[_name] = S_ALL
    S_ALL += _size


def nt(a, b, precision=None):
    return lax.dot_general(
        a, b, (((1,), (1,)), ((), ())), preferred_element_type=F32, precision=precision
    )


def high(a, b):
    return jnp.dot(a, b, precision=HI, preferred_element_type=F32)


def coded(v, axis):
    most = jnp.maximum(jnp.max(v, axis=axis, keepdims=True), 1e-30)
    return jnp.round(v * (TOP / most)).astype(jnp.int32).astype(I16), most


def decoded(q, most):
    return q.astype(jnp.int32).astype(F32) * (most * (1.0 / TOP))


def kernel(
    counts, w1, h1, w2t, h2,
    w1_out, hbuf, w2t_out, h2b,
    wg, cnt, h1v, w2tv, h2v, hl, num, nq, nqr, nm, nmr, cs,
    e1s, e1r, part, acc, pq, pqr, ps, psr, aq, aqr, aps, apr, fin, lq, lqr, lps, lpr,
    sm, smr, sv, svr, sz, szr, sx, sy, sg,
    snd, rcv, loc,
):
    g = lax.axis_index("gene")
    ci = lax.axis_index("cell")
    mx, my, mz, mc = ci // 16, (ci // 4) % 4, (ci // 2) % 2, ci % 2
    oz, oc = 1 - mz, 1 - mc

    def cell(x, y, z, c):
        return ((x * NY + y) * NZ + z) * NC + c

    def at_x(d):
        return (mx + d) % NX

    def at_y(d):
        return (my + d) % NY

    def at_g(d):
        return (g + d) % NG

    def copy(src, dst, name, k, to):
        sem = PLACE[name] + k
        return pltpu.make_async_remote_copy(
            src_ref=src,
            dst_ref=dst,
            send_sem=snd.at[sem],
            recv_sem=rcv.at[sem],
            device_id=to,
            device_id_type=pl.DeviceIdType.MESH,
        )

    sibling = (g, cell(mx, my, mz, oc))
    z_pair = (g, cell(mx, my, oz, mc))

    def to_x(d):
        return (g, cell(at_x(d), my, mz, mc))

    def to_y(d):
        return (g, cell(mx, at_y(d), mz, mc))

    def to_g(d):
        return (at_g(d), ci)

    own = wg.at[mx, my, mz, mc]
    barrier = pltpu.get_barrier_semaphore()
    partners = [sibling, z_pair]
    for d in range(1, 4):
        partners += [to_x(d), to_y(d), to_g(d)]
    for to in partners:
        pl.semaphore_signal(barrier, inc=1, device_id=to, device_id_type=pl.DeviceIdType.MESH)
    read_w1 = pltpu.make_async_copy(w1, own, loc.at[0])
    read_h1 = pltpu.make_async_copy(h1, h1v, loc.at[1])
    read_w2 = pltpu.make_async_copy(w2t, w2tv, loc.at[2])
    read_h2 = pltpu.make_async_copy(h2, h2v, loc.at[3])
    read_counts = pltpu.make_async_copy(counts, cnt, loc.at[4])
    for read in (read_w1, read_h1, read_w2, read_h2, read_counts):
        read.start()
    read_w1.wait()
    pl.semaphore_wait(barrier, len(partners))

    go_z = copy(own, own, "z", 0, z_pair)
    go_z.start()
    read_h1.wait()
    hl[...] = h1v[...].astype(BF16)
    num[...] = jnp.zeros_like(num)
    cs[...] = jnp.zeros_like(cs)
    go_z.wait_recv()

    def stage_two(h, d):
        src = wg.at[mx, my, :, mc, h]
        return copy(src, src, "a2", 3 * h + d - 1, to_x(d) if h == 0 else to_y(d))

    for d in ORDER:
        for h in range(2):
            stage_two(h, d).start()
    for d in ORDER:
        for h in range(2):
            stage_two(h, d).wait_recv()

    def column(h, d):
        return wg.at[:, at_y(4 - d), :, mc, 0] if h == 0 else wg.at[at_x(4 - d), :, :, mc, 1]

    def stage_three(h, d):
        src = column(h, 0)
        return copy(src, src, "a3", 3 * h + d - 1, to_y(d) if h == 0 else to_x(d))

    def forward(h, d):
        src = column(h, d)
        return copy(src, src, "f", 4 * h + d, sibling)

    for d in ORDER:
        for h in range(2):
            stage_three(h, d).start()
    for h in range(2):
        forward(h, 0).start()

    read_counts.wait()

    def pass_on(d):
        for h in range(2):
            stage_three(h, d).wait_recv()
            forward(h, d).start()

    def first(w, v):
        approx = jnp.dot(w, hl[...], preferred_element_type=F32)
        ratio = (v.astype(F32) / approx).astype(BF16)
        add = lax.dot_general(
            w, ratio, (((0,), (0,)), ((), ())), preferred_element_type=F32
        )
        for j in range(NG):
            num[j] += add[:, j * 128 : (j + 1) * 128]
        cs[...] += jnp.sum(w.astype(F32).reshape(-1, 8, w.shape[1]), axis=0)

    def first_step(t, carry):
        d = t + t // 2 - 2 * (t // 3)
        forward(0, d).wait_recv()
        first(
            wg[:, at_y(4 - d), :, :, 0].reshape(512, 512),
            cnt[:, at_y(4 - d), :, :, 0].reshape(512, 512),
        )
        forward(1, d).wait_recv()
        first(
            wg[at_x(4 - d), :, :, :, 1].reshape(512, 512),
            cnt[at_x(4 - d), :, :, :, 1].reshape(512, 512),
        )

        @pl.when(t == 0)
        def _():
            pass_on(1)
            pass_on(3)

        @pl.when(t == 1)
        def _():
            pass_on(2)

        return carry

    lax.fori_loop(0, 4, first_step, 0)

    def send_num(d):
        return copy(nq.at[d - 1], nqr.at[d - 1], "n", d - 1, to_g(d))

    def send_marks(d):
        return copy(nm.at[d - 1], nmr.at[d - 1], "m", d - 1, to_g(d))

    for d in ORDER:
        q, most = coded(num[at_g(d)], 0)
        nq[d - 1] = q
        send_num(d).start()
        nm[d - 1, :, 0:512] = cs[...]
        nm[d - 1, :, 512:640] = jnp.broadcast_to(most, (8, 128))
        send_marks(d).start()
    read_w2.wait()
    read_h2.wait()
    w2 = jnp.transpose(w2tv[...])
    mine = pl.ds(pl.multiple_of(g * 128, 128), 128)
    h2_mine = h2v[:, mine]
    fit = high(w2, h2_mine)
    for d in ORDER:
        send_marks(d).wait_recv()
    parts = cs[...] + nmr[0, :, 0:512] + nmr[1, :, 0:512] + nmr[2, :, 0:512]
    total = jnp.sum(parts, axis=0, keepdims=True)
    colsum = jnp.transpose(jnp.broadcast_to(total, (128, 512)))
    h1_num = num[g]
    for d in ORDER:
        send_num(d).wait_recv()
        h1_num += decoded(nqr[d - 1], nmr[d - 1, 0:1, 512:640])
    fresh = h1v[:, mine] * h1_num / colsum
    top = fresh.astype(BF16)
    hbuf[0, g] = top
    hbuf[1, g] = (fresh - top.astype(F32)).astype(BF16)

    def send_h(h, d):
        src = hbuf.at[h, g]
        return copy(src, src, "hb", 3 * h + d - 1, to_g(d))

    for d in ORDER:
        send_h(0, d).start()

    ratio3 = fresh / fit
    lift = high(w2tv[...], ratio3)
    h2_new = h2_mine * lift / jnp.sum(w2tv[...], axis=1, keepdims=True)
    h2b[g] = h2_new
    ratio4 = fresh / high(w2, h2_new)
    w2_part = nt(h2_new, ratio4, HI)
    h2_part = jnp.broadcast_to(jnp.sum(h2_new, axis=1, keepdims=True), (64, 128))
    rows = nt(jnp.ones((8, 128), F32), fresh, HI)
    for j in range(NG):
        for c in range(NC):
            at = 16 * j + 8 * c
            sm[j, c, :, 0:512] = w2_part[at : at + 8]
            sm[j, c, :, 512:640] = h2_part[at : at + 8]
            sm[j, c, :, 640:768] = jnp.zeros((8, 128), F32)
            for k in range(4):
                sm[j, c, k : k + 1, 640:768] = rows[0:1, k * 128 : (k + 1) * 128]

    def sum_g(d):
        return copy(sm.at[at_g(d)], smr.at[d - 1], "s0", d - 1, to_g(d))

    sum_c = copy(sv.at[oc], svr, "s1", 0, sibling)
    sum_z = copy(sz, szr, "s2", 0, z_pair)

    def sum_x(d):
        return copy(sx.at[mx], sx.at[mx], "s3", d - 1, to_x(d))

    def sum_y(d):
        return copy(sy.at[my], sy.at[my], "s4", d - 1, to_y(d))

    def all_g(d):
        return copy(sg.at[mc, g], sg.at[mc, g], "s5", d - 1, to_g(d))

    all_c = copy(sg.at[mc], sg.at[mc], "s6", 0, sibling)

    def send_h2(d):
        return copy(h2b.at[g], h2b.at[g], "h2", d - 1, to_g(d))

    for d in ORDER:
        sum_g(d).start()
    for d in ORDER:
        send_h2(d).start()
    for d in ORDER:
        send_h(0, d).wait_recv()
    for j in range(NG):
        hl[:, j * 128 : (j + 1) * 128] = hbuf[0, j]

    def second(w, v):
        approx = jnp.dot(w, hl[...], preferred_element_type=F32)
        ratio = (v.astype(F32) / approx).astype(BF16)
        return nt(ratio, hl[...]).reshape(4, 2, 32, 512)

    def pick(ref, h, i, c):
        d = i + 1
        found = ref[at_x(d), :, :, c, 0] if h == 0 else ref[:, at_y(d), :, c, 1]
        return found.reshape(256, 512)

    def to_sibling(h, i):
        return copy(e1s.at[h, i], e1r.at[h, i], "e1", 4 * h + i, sibling)

    def along(h, i):
        to = to_x(i + 1) if h == 0 else to_y(i + 1)
        return (
            copy(pq.at[h, i], pqr.at[h, i], "p", 3 * h + i, to),
            copy(ps.at[h, i], psr.at[h, i], "ps", 3 * h + i, to),
        )

    def second_step(i, carry):
        for h in range(2):
            e1s[h, i] = second(pick(wg, h, i, oc), pick(cnt, h, i, oc))
            to_sibling(h, i).start()
        for h in range(2):
            part[h] = second(pick(wg, h, i, mc), pick(cnt, h, i, mc))
        for h in range(2):
            to_sibling(h, i).wait_recv()

            @pl.when(i < 3)
            def _():
                q, most = coded((part[h] + e1r[h, i]).reshape(8, 32, 512), 1)
                pq[h, i] = q.reshape(4, 2, 32, 512)
                ps[h, i] = most.reshape(8, 512)
                for go in along(h, i):
                    go.start()

            @pl.when(i == 3)
            def _():
                acc[h] = part[h] + e1r[h, 3]

        @pl.when(i == 0)
        def _():
            for d in ORDER:
                sum_g(d).wait_recv()
            sv[...] = sm[g] + smr[0] + smr[1] + smr[2]
            sum_c.start()
            for d in ORDER:
                send_h(1, d).start()

        @pl.when(i == 1)
        def _():
            sum_c.wait_recv()
            sz[...] = sv[mc] + svr[...]
            sum_z.start()

        @pl.when(i == 2)
        def _():
            sum_z.wait_recv()
            sx[mx] = sz[...] + szr[...]
            for d in ORDER:
                sum_x(d).start()

        @pl.when(i == 3)
        def _():
            for d in ORDER:
                sum_x(d).wait_recv()
            sy[my] = sx[0] + sx[1] + sx[2] + sx[3]
            for d in ORDER:
                sum_y(d).start()

        return carry

    lax.fori_loop(0, 4, second_step, 0)

    def across(h, d):
        to = to_y(d) if h == 0 else to_x(d)
        k = 3 * h + d - 1
        return (
            copy(aq.at[h, d - 1], aqr.at[h, d - 1], "q", k, to),
            copy(aps.at[h, d - 1], apr.at[h, d - 1], "qs", k, to),
        )

    for h in range(2):
        for i in (0, 2, 1):
            for go in along(h, i):
                go.wait_recv()
        whole = acc[h].reshape(8, 32, 512)
        for i in range(3):
            whole += decoded(pqr[h, i].reshape(8, 32, 512), psr[h, i].reshape(8, 1, 512))
        acc[h] = whole.reshape(4, 2, 32, 512)
        for d in ORDER:
            q, most = coded(acc[h, at_y(d) if h == 0 else at_x(d)], 1)
            aq[h, d - 1] = q
            aps[h, d - 1] = jnp.broadcast_to(most, (2, 8, 512))
            for go in across(h, d):
                go.start()
    for d in ORDER:
        sum_y(d).wait_recv()
    done = sy[0] + sy[1] + sy[2] + sy[3]
    sg[mc, g] = done
    for d in ORDER:
        all_g(d).start()
    for h in range(2):
        for d in ORDER:
            for go in across(h, d):
                go.wait_recv()
        whole = acc[h, my if h == 0 else mx]
        for k in range(3):
            whole += decoded(aqr[h, k], apr[h, k, :, 0:1])
        fin[:, h] = whole
    q, most = coded(fin[oz], 1)
    lq[...] = q
    lps[...] = jnp.broadcast_to(most, (2, 8, 512))
    last = (copy(lq, lqr, "l", 0, z_pair), copy(lps, lpr, "ls", 0, z_pair))
    for go in last:
        go.start()
    for d in ORDER:
        all_g(d).wait_recv()
    all_c.start()
    rowsum = jnp.concatenate([done[k : k + 1, 640:768] for k in range(4)], axis=1)
    for go in last:
        go.wait_recv()
    w1_num = (fin[mz] + decoded(lqr[...], lpr[:, 0:1])).reshape(64, 512)
    w1_now = wg[mx, my, mz, mc].astype(F32).reshape(64, 512)
    w1_out[...] = (w1_now * w1_num / rowsum).astype(BF16)
    all_c.wait_recv()
    for j in range(NG):
        for c in range(NC):
            at = slice(16 * j + 8 * c, 16 * j + 8 * c + 8)
            w2t_out[at, :] = w2tv[at, :] * sg[c, j, :, 0:512] / sg[c, j, :, 512:513]

    for d in ORDER:
        send_h(1, d).wait_recv()
        send_h2(d).wait_recv()
    for sent in (go_z, sum_c, sum_z, all_c) + last:
        sent.wait_send()
    for d in ORDER:
        for h in range(2):
            for sent in (stage_two(h, d), stage_three(h, d), send_h(h, d)):
                sent.wait_send()
            for sent in along(h, d - 1) + across(h, d):
                sent.wait_send()
        for sent in (send_num, send_marks, send_h2, sum_g, sum_x, sum_y, all_g):
            sent(d).wait_send()
    for h in range(2):
        for d in range(4):
            forward(h, d).wait_send()
            to_sibling(h, d).wait_send()


def finish(w1, hbuf, w2t, h2b, w1_out, h1_out, w2t_out, h2_out):
    w1_out[...] = w1[...]
    w2t_out[...] = w2t[...]
    for j in range(NG):
        at = slice(j * 128, (j + 1) * 128)
        h1_out[:, at] = hbuf[0, j].astype(F32) + hbuf[1, j].astype(F32)
        h2_out[:, at] = h2b[j]


def on_device(counts, w1, h1, w2, h2):
    vmem = pl.BlockSpec(memory_space=pltpu.VMEM)
    shape = (NX, NY, NZ, NC, 2, 32, 512)
    sds = jax.ShapeDtypeStruct
    scratch = [
        (shape, BF16), (shape, jnp.int32), ((512, 512), F32), ((64, 512), F32), ((64, 512), F32),
        ((512, 512), BF16), ((NG, 512, 128), F32), ((3, 512, 128), I16), ((3, 512, 128), I16),
        ((3, 8, 640), F32), ((3, 8, 640), F32), ((8, 512), F32),
        ((2, 4, 4, 2, 32, 512), F32), ((2, 4, 4, 2, 32, 512), F32),
        ((2, 4, 2, 32, 512), F32), ((2, 4, 2, 32, 512), F32),
        ((2, 3, 4, 2, 32, 512), I16), ((2, 3, 4, 2, 32, 512), I16), ((2, 3, 8, 512), F32), ((2, 3, 8, 512), F32),
        ((2, 3, 2, 32, 512), I16), ((2, 3, 2, 32, 512), I16), ((2, 3, 2, 8, 512), F32), ((2, 3, 2, 8, 512), F32),
        ((2, 2, 32, 512), F32), ((2, 32, 512), I16), ((2, 32, 512), I16), ((2, 8, 512), F32), ((2, 8, 512), F32),
        ((NG, 2, 8, 768), F32), ((3, 2, 8, 768), F32), ((2, 8, 768), F32), ((8, 768), F32),
        ((8, 768), F32), ((8, 768), F32), ((4, 8, 768), F32), ((4, 8, 768), F32), ((2, NG, 8, 768), F32),
    ]
    moved = pl.pallas_call(
        kernel,
        out_shape=(
            sds((64, 512), BF16),
            sds((2, NG, 512, 128), BF16),
            sds((64, 512), F32),
            sds((NG, 64, 128), F32),
        ),
        in_specs=[pl.BlockSpec(memory_space=pl.ANY)] * 5,
        out_specs=(vmem,) * 4,
        scratch_shapes=[pltpu.VMEM(*s) for s in scratch]
        + [
            pltpu.SemaphoreType.DMA((S_ALL,)),
            pltpu.SemaphoreType.DMA((S_ALL,)),
            pltpu.SemaphoreType.DMA((5,)),
        ],
        compiler_params=pltpu.CompilerParams(
            collective_id=0, has_side_effects=True, vmem_limit_bytes=56 * 1024 * 1024
        ),
    )(counts.reshape(shape), w1.reshape(2, 32, 512), h1, w2.T, h2)
    w1_new, h1_new, w2t_new, h2_new = pl.pallas_call(
        finish,
        out_shape=(
            sds((64, 512), BF16),
            sds((512, 512), F32),
            sds((64, 512), F32),
            sds((64, 512), F32),
        ),
        in_specs=[vmem] * 4,
        out_specs=(vmem,) * 4,
    )(*moved)
    return w1_new, h1_new, w2t_new.T, h2_new


def solution(mesh):
    placed = (P("gene", "cell"), P(("gene", "cell"), None), P(None, "cell"), P(), P(None, "cell"))
    return jax.shard_map(
        on_device,
        mesh=mesh,
        in_specs=placed,
        out_specs=(P(("gene", "cell"), None), P(None, "cell"), P(), P(None, "cell")),
        check_vma=False,
    )
```

```python
import jax
import jax.numpy as jnp
from jax import lax
from jax.experimental import pallas as pl
from jax.experimental.pallas import tpu as pltpu
from jax.sharding import PartitionSpec as P

NX, NY, NZ, NC = 4, 4, 2, 2
NG = 4
F32, BF16, I16 = jnp.float32, jnp.bfloat16, jnp.int16
HI = lax.Precision.HIGHEST
TOP = 32767.0
ORDER = (1, 3, 2)

SIZES = dict(
    z=1, a2=12, a3=18, f=8, m=3, n=6, hb=6, hs=6, h2=3, e1=8, p=6, ps=6, q=6, qs=6, l=1, ls=1,
    s0=1, s1=3, s2=1, s3=3, s4=3, s5=3, s6=1,
)
PLACE, S_ALL = {}, 0
for _name, _size in SIZES.items():
    PLACE[_name] = S_ALL
    S_ALL += _size


def nt(a, b, precision=None):
    return lax.dot_general(
        a, b, (((1,), (1,)), ((), ())), preferred_element_type=F32, precision=precision
    )


def high(a, b):
    return jnp.dot(a, b, precision=HI, preferred_element_type=F32)


def most_of(v, axis):
    return jnp.maximum(jnp.max(v, axis=axis, keepdims=True), 1e-30)


def coded(v, most):
    return jnp.round(v * (TOP / most)).astype(jnp.int32).astype(I16)


def decoded(q, most):
    return q.astype(jnp.int32).astype(F32) * (most * (1.0 / TOP))


def kernel(
    counts, w1, h1, w2t, h2,
    w1_out, h1_out, w2t_out, h2_out,
    wg, cnt, h1v, w2tv, h2v, hl, num, nq, nqr, nm, nmr, cs, fr, hq, hs, h1f, h2b,
    rb, e1r, acc, pq, pqr, ps, psr, aq, aqr, aps, apr, fin, lq, lqr, lps, lpr,
    sm, smr, sv, svr, sz, szr, sx, sy, sg, w1f, w2f,
    snd, rcv, loc,
):
    g = lax.axis_index("gene")
    ci = lax.axis_index("cell")
    mx, my, mz, mc = ci // 16, (ci // 4) % 4, (ci // 2) % 2, ci % 2
    oz, oc = 1 - mz, 1 - mc

    def cell(x, y, z, c):
        return ((x * NY + y) * NZ + z) * NC + c

    def at_x(d):
        return (mx + d) % NX

    def at_y(d):
        return (my + d) % NY

    def at_g(d):
        return (g + d) % NG

    def copy(src, dst, name, k, to):
        sem = PLACE[name] + k
        return pltpu.make_async_remote_copy(
            src_ref=src,
            dst_ref=dst,
            send_sem=snd.at[sem],
            recv_sem=rcv.at[sem],
            device_id=to,
            device_id_type=pl.DeviceIdType.MESH,
        )

    sibling = (g, cell(mx, my, mz, oc))
    z_pair = (g, cell(mx, my, oz, mc))

    def to_x(d):
        return (g, cell(at_x(d), my, mz, mc))

    def to_y(d):
        return (g, cell(mx, at_y(d), mz, mc))

    def to_g(d):
        return (at_g(d), ci)

    own = wg.at[mx, my, mz, mc]
    barrier = pltpu.get_barrier_semaphore()
    partners = [sibling, z_pair]
    for d in range(1, 4):
        partners += [to_x(d), to_y(d), to_g(d)]
    for to in partners:
        pl.semaphore_signal(barrier, inc=1, device_id=to, device_id_type=pl.DeviceIdType.MESH)
    read_w1 = pltpu.make_async_copy(w1, own, loc.at[0])
    read_h1 = pltpu.make_async_copy(h1, h1v, loc.at[1])
    read_w2 = pltpu.make_async_copy(w2t, w2tv, loc.at[2])
    read_h2 = pltpu.make_async_copy(h2, h2v, loc.at[3])
    read_counts = pltpu.make_async_copy(counts, cnt, loc.at[4])
    for read in (read_w1, read_h1, read_w2, read_h2, read_counts):
        read.start()
    read_w1.wait()
    pl.semaphore_wait(barrier, len(partners))

    go_z = copy(own, own, "z", 0, z_pair)
    go_z.start()

    def near(k, a, d):
        src = wg.at[mx, my, oz if k else mz, mc]
        return copy(src, src, "a2", 6 * k + 3 * a + d - 1, to_y(d) if a else to_x(d))

    for d in ORDER:
        for a in range(2):
            near(0, a, d).start()
    read_h1.wait()
    hl[...] = h1v[...].astype(BF16)
    num[...] = jnp.zeros_like(num)
    cs[...] = jnp.zeros_like(cs)
    go_z.wait_recv()
    for d in ORDER:
        for a in range(2):
            near(1, a, d).start()

    def column(h, d):
        return wg.at[:, at_y(4 - d), :, mc, 0] if h == 0 else wg.at[at_x(4 - d), :, :, mc, 1]

    def far(h, e, d):
        src = wg.at[mx, at_y(4 - e), :, mc, 1] if h else wg.at[at_x(4 - e), my, :, mc, 0]
        return copy(src, src, "a3", 9 * h + 3 * (e - 1) + d - 1, to_x(d) if h else to_y(d))

    def forward(h, d):
        src = column(h, d)
        return copy(src, src, "f", 4 * h + d, sibling)

    for e in ORDER:
        for h in range(2):
            near(0, h, e).wait_recv()
            near(1, h, e).wait_recv()
            for d in ORDER:
                far(h, e, d).start()
    for h in range(2):
        forward(h, 0).start()

    read_counts.wait()

    def pass_on(d):
        for h in range(2):
            for e in ORDER:
                far(h, e, d).wait_recv()
            forward(h, d).start()

    def first(w, v):
        approx = jnp.dot(w, hl[...], preferred_element_type=F32)
        ratio = (v.astype(F32) / approx).astype(BF16)
        add = lax.dot_general(
            w, ratio, (((0,), (0,)), ((), ())), preferred_element_type=F32
        )
        for j in range(NG):
            num[j] += add[:, j * 128 : (j + 1) * 128]
        cs[...] += jnp.sum(w.astype(F32).reshape(-1, 8, w.shape[1]), axis=0)

    def first_step(t, carry):
        d = t + t // 2 - 2 * (t // 3)
        forward(0, d).wait_recv()
        first(
            wg[:, at_y(4 - d), :, :, 0].reshape(512, 512),
            cnt[:, at_y(4 - d), :, :, 0].reshape(512, 512),
        )
        forward(1, d).wait_recv()
        first(
            wg[at_x(4 - d), :, :, :, 1].reshape(512, 512),
            cnt[at_x(4 - d), :, :, :, 1].reshape(512, 512),
        )

        @pl.when(t == 0)
        def _():
            pass_on(1)
            pass_on(3)

        @pl.when(t == 1)
        def _():
            pass_on(2)

        return carry

    lax.fori_loop(0, 4, first_step, 0)

    def block(b):
        return pl.ds(256 * b, 256)

    def send_num(b, d):
        return copy(nq.at[d - 1, block(b)], nqr.at[d - 1, block(b)], "n", 3 * b + d - 1, to_g(d))

    def send_marks(d):
        return copy(nm.at[d - 1], nmr.at[d - 1], "m", d - 1, to_g(d))

    def send_h(b, d):
        k = 3 * b + d - 1
        return (
            copy(hq.at[b, g], hq.at[b, g], "hb", k, to_g(d)),
            copy(hs.at[b, g], hs.at[b, g], "hs", k, to_g(d)),
        )

    for d in ORDER:
        most = most_of(num[at_g(d)], 0)
        nm[d - 1, :, 0:512] = cs[...]
        nm[d - 1, :, 512:640] = jnp.broadcast_to(most, (8, 128))
        send_marks(d).start()
        nq[d - 1, 0:256] = coded(num[at_g(d), 0:256], most)
        send_num(0, d).start()
    for d in ORDER:
        nq[d - 1, 256:512] = coded(num[at_g(d), 256:512], nm[d - 1, 0:1, 512:640])
        send_num(1, d).start()
    read_w2.wait()
    read_h2.wait()
    w2 = jnp.transpose(w2tv[...])
    mine = pl.ds(pl.multiple_of(g * 128, 128), 128)
    h2_mine = h2v[:, mine]
    fit = high(w2, h2_mine)
    for d in ORDER:
        send_marks(d).wait_recv()
    parts = cs[...] + nmr[0, :, 0:512] + nmr[1, :, 0:512] + nmr[2, :, 0:512]
    total = jnp.sum(parts, axis=0, keepdims=True)
    colsum = jnp.transpose(jnp.broadcast_to(total, (128, 512)))
    for b in range(2):
        at = slice(256 * b, 256 * b + 256)
        h1_num = num[g, at]
        for d in ORDER:
            send_num(b, d).wait_recv()
            h1_num += decoded(nqr[d - 1, at], nmr[d - 1, 0:1, 512:640])
        new = h1v[at, mine] * h1_num / colsum[at]
        fr[at] = new
        most = most_of(new, 0)
        hq[b, g] = coded(new, most)
        hs[b, g] = jnp.broadcast_to(most, (8, 128))
        for d in ORDER:
            for go in send_h(b, d):
                go.start()
    fresh = fr[...]

    ratio3 = fresh / fit
    lift = high(w2tv[...], ratio3)
    h2_new = h2_mine * lift / jnp.sum(w2tv[...], axis=1, keepdims=True)
    h2b[g] = h2_new
    ratio4 = fresh / high(w2, h2_new)
    w2_part = nt(h2_new, ratio4, HI)
    h2_part = jnp.broadcast_to(jnp.sum(h2_new, axis=1, keepdims=True), (64, 128))
    rows = nt(jnp.ones((8, 128), F32), fresh, HI)
    for j in range(NG):
        for c in range(NC):
            at = 16 * j + 8 * c
            sm[c, j, :, 0:512] = w2_part[at : at + 8]
            sm[c, j, :, 512:640] = h2_part[at : at + 8]
            sm[c, j, :, 640:768] = jnp.zeros((8, 128), F32)
            for k in range(4):
                sm[c, j, k : k + 1, 640:768] = rows[0:1, k * 128 : (k + 1) * 128]

    sum_c = copy(sm.at[oc], smr, "s0", 0, sibling)

    def sum_g(d):
        return copy(sv.at[at_g(d)], svr.at[d - 1], "s1", d - 1, to_g(d))

    sum_z = copy(sz, szr, "s2", 0, z_pair)

    def sum_x(d):
        return copy(sx.at[mx], sx.at[mx], "s3", d - 1, to_x(d))

    def sum_y(d):
        return copy(sy.at[my], sy.at[my], "s4", d - 1, to_y(d))

    def all_g(d):
        return copy(sg.at[mc, g], sg.at[mc, g], "s5", d - 1, to_g(d))

    all_c = copy(sg.at[mc], sg.at[mc], "s6", 0, sibling)

    def send_h2(d):
        return copy(h2b.at[g], h2b.at[g], "h2", d - 1, to_g(d))

    sum_c.start()
    for b in range(2):
        for d in (0,) + ORDER:
            if d:
                for go in send_h(b, d):
                    go.wait_recv()
            j = at_g(4 - d)
            value = decoded(hq[b, j], hs[b, j, 0:1])
            there = pl.ds(pl.multiple_of(j * 128, 128), 128)
            h1f[block(b), there] = value
            hl[block(b), there] = value.astype(BF16)
        if b == 0:
            sum_c.wait_recv()
            sv[...] = sm[mc] + smr[...]
            for d in ORDER:
                sum_g(d).start()

    def second(h, i):
        d = i + 1
        w = wg[:, at_y(d), :, :, 1] if h else wg[at_x(d), :, :, :, 0]
        v = cnt[:, at_y(d), :, :, 1] if h else cnt[at_x(d), :, :, :, 0]
        approx = jnp.dot(w.reshape(512, 512), hl[...], preferred_element_type=F32)
        ratio = (v.reshape(512, 512).astype(F32) / approx).astype(BF16)
        rb[h, i] = nt(ratio, hl[...]).reshape(4, 2, 2, 32, 512)

    def to_sibling(h, i):
        return copy(rb.at[h, i, :, :, oc], e1r.at[h, i], "e1", 4 * h + i, sibling)

    def along(h, i):
        to = to_x(i + 1) if h == 0 else to_y(i + 1)
        return (
            copy(pq.at[h, i], pqr.at[h, i], "p", 3 * h + i, to),
            copy(ps.at[h, i], psr.at[h, i], "ps", 3 * h + i, to),
        )

    def add_up(h, i):
        to_sibling(h, i).wait_recv()
        both = rb[h, i, :, :, mc] + e1r[h, i]

        @pl.when(i < 3)
        def _():
            v = both.reshape(8, 32, 512)
            most = most_of(v, 1)
            pq[h, i] = coded(v, most).reshape(4, 2, 32, 512)
            ps[h, i] = most.reshape(8, 512)
            for go in along(h, i):
                go.start()

        @pl.when(i == 3)
        def _():
            acc[h] = both

    def second_step(i, carry):
        @pl.when(i < 4)
        def _():
            for h in range(2):
                second(h, i)
                to_sibling(h, i).start()

        @pl.when(i > 0)
        def _():
            for h in range(2):
                add_up(h, i - 1)

        @pl.when(i == 2)
        def _():
            for d in ORDER:
                sum_g(d).wait_recv()
            sz[...] = sv[g] + svr[0] + svr[1] + svr[2]
            sum_z.start()
            for d in ORDER:
                send_h2(d).start()

        @pl.when(i == 4)
        def _():
            sum_z.wait_recv()
            sx[mx] = sz[...] + szr[...]
            for d in ORDER:
                sum_x(d).start()

        return carry

    lax.fori_loop(0, 5, second_step, 0)
    put_h1 = pltpu.make_async_copy(h1f, h1_out, loc.at[5])
    put_h1.start()

    def across(h, d):
        to = to_y(d) if h == 0 else to_x(d)
        k = 3 * h + d - 1
        return (
            copy(aq.at[h, d - 1], aqr.at[h, d - 1], "q", k, to),
            copy(aps.at[h, d - 1], apr.at[h, d - 1], "qs", k, to),
        )

    for h in range(2):
        for i in (0, 2, 1):
            for go in along(h, i):
                go.wait_recv()
        whole = acc[h].reshape(8, 32, 512)
        for i in range(3):
            whole += decoded(pqr[h, i].reshape(8, 32, 512), psr[h, i].reshape(8, 1, 512))
        acc[h] = whole.reshape(4, 2, 32, 512)
        for d in ORDER:
            v = acc[h, at_y(d) if h == 0 else at_x(d)]
            most = most_of(v, 1)
            aq[h, d - 1] = coded(v, most)
            aps[h, d - 1] = jnp.broadcast_to(most, (2, 8, 512))
            for go in across(h, d):
                go.start()
    for d in ORDER:
        sum_x(d).wait_recv()
    sy[my] = sx[0] + sx[1] + sx[2] + sx[3]
    for d in ORDER:
        sum_y(d).start()
    for d in ORDER:
        sum_y(d).wait_recv()
    done = sy[0] + sy[1] + sy[2] + sy[3]
    sg[mc, g] = done
    for d in ORDER:
        all_g(d).start()
    for h in range(2):
        for d in ORDER:
            for go in across(h, d):
                go.wait_recv()
        whole = acc[h, my if h == 0 else mx]
        for k in range(3):
            whole += decoded(aqr[h, k], apr[h, k, :, 0:1])
        fin[:, h] = whole
    most = most_of(fin[oz], 1)
    lq[...] = coded(fin[oz], most)
    lps[...] = jnp.broadcast_to(most, (2, 8, 512))
    last = (copy(lq, lqr, "l", 0, z_pair), copy(lps, lpr, "ls", 0, z_pair))
    for go in last:
        go.start()
    for d in ORDER:
        all_g(d).wait_recv()
    all_c.start()
    for d in ORDER:
        send_h2(d).wait_recv()
    puts = [
        pltpu.make_async_copy(h2b.at[j], h2_out.at[:, 128 * j : 128 * j + 128], loc.at[6 + j])
        for j in range(NG)
    ]
    for put in puts:
        put.start()
    rowsum = jnp.concatenate([done[k : k + 1, 640:768] for k in range(4)], axis=1)
    for go in last:
        go.wait_recv()
    w1_num = (fin[mz] + decoded(lqr[...], lpr[:, 0:1])).reshape(64, 512)
    w1_now = wg[mx, my, mz, mc].astype(F32).reshape(64, 512)
    w1f[...] = (w1_now * w1_num / rowsum).astype(BF16)
    puts.append(pltpu.make_async_copy(w1f, w1_out, loc.at[10]))
    puts[-1].start()
    all_c.wait_recv()
    for j in range(NG):
        for c in range(NC):
            at = slice(16 * j + 8 * c, 16 * j + 8 * c + 8)
            w2f[at, :] = w2tv[at, :] * sg[c, j, :, 0:512] / sg[c, j, :, 512:513]

    puts.append(pltpu.make_async_copy(w2f, w2t_out, loc.at[11]))
    puts[-1].start()

    for sent in (go_z, sum_c, sum_z, all_c) + last:
        sent.wait_send()
    for d in ORDER:
        for h in range(2):
            for sent in (near(0, h, d), near(1, h, d), send_num(h, d)) + send_h(h, d):
                sent.wait_send()
            for e in ORDER:
                far(h, e, d).wait_send()
            for sent in along(h, d - 1) + across(h, d):
                sent.wait_send()
        for sent in (send_marks, send_h2, sum_g, sum_x, sum_y, all_g):
            sent(d).wait_send()
    for h in range(2):
        for d in range(4):
            forward(h, d).wait_send()
            to_sibling(h, d).wait_send()
    for put in puts + [put_h1]:
        put.wait()


def finish(*refs):
    *arrays, sem = refs
    copies = [
        pltpu.make_async_copy(arrays[k], arrays[k + 4], sem.at[k]) for k in range(4)
    ]
    for go in copies:
        go.start()
    for go in copies:
        go.wait()


def on_device(counts, w1, h1, w2, h2):
    anywhere = pl.BlockSpec(memory_space=pl.ANY)
    shape = (NX, NY, NZ, NC, 2, 32, 512)
    sds = jax.ShapeDtypeStruct
    outs = (
        sds((64, 512), BF16),
        sds((512, 512), F32),
        sds((64, 512), F32),
        sds((64, 512), F32),
    )
    scratch = [
        (shape, BF16), (shape, jnp.int32), ((512, 512), F32), ((64, 512), F32), ((64, 512), F32),
        ((512, 512), BF16), ((NG, 512, 128), F32), ((3, 512, 128), I16), ((3, 512, 128), I16),
        ((3, 8, 640), F32), ((3, 8, 640), F32), ((8, 512), F32),
        ((512, 128), F32), ((2, NG, 256, 128), I16), ((2, NG, 8, 128), F32), ((512, 512), F32), ((NG, 64, 128), F32),
        ((2, 4, 4, 2, 2, 32, 512), F32), ((2, 4, 4, 2, 32, 512), F32), ((2, 4, 2, 32, 512), F32),
        ((2, 3, 4, 2, 32, 512), I16), ((2, 3, 4, 2, 32, 512), I16), ((2, 3, 8, 512), F32), ((2, 3, 8, 512), F32),
        ((2, 3, 2, 32, 512), I16), ((2, 3, 2, 32, 512), I16), ((2, 3, 2, 8, 512), F32), ((2, 3, 2, 8, 512), F32),
        ((2, 2, 32, 512), F32), ((2, 32, 512), I16), ((2, 32, 512), I16), ((2, 8, 512), F32), ((2, 8, 512), F32),
        ((2, NG, 8, 768), F32), ((NG, 8, 768), F32), ((NG, 8, 768), F32), ((3, 8, 768), F32), ((8, 768), F32),
        ((8, 768), F32), ((4, 8, 768), F32), ((4, 8, 768), F32), ((2, NG, 8, 768), F32),
        ((64, 512), BF16), ((64, 512), F32),
    ]
    moved = pl.pallas_call(
        kernel,
        out_shape=outs,
        in_specs=[anywhere] * 5,
        out_specs=(anywhere,) * 4,
        scratch_shapes=[pltpu.VMEM(*s) for s in scratch]
        + [
            pltpu.SemaphoreType.DMA((S_ALL,)),
            pltpu.SemaphoreType.DMA((S_ALL,)),
            pltpu.SemaphoreType.DMA((12,)),
        ],
        compiler_params=pltpu.CompilerParams(
            collective_id=0, has_side_effects=True, vmem_limit_bytes=56 * 1024 * 1024
        ),
    )(counts.reshape(shape), w1.reshape(2, 32, 512), h1, w2.T, h2)
    w1_new, h1_new, w2t_new, h2_new = pl.pallas_call(
        finish,
        out_shape=outs,
        in_specs=[anywhere] * 4,
        out_specs=(anywhere,) * 4,
        scratch_shapes=[pltpu.SemaphoreType.DMA((4,))],
    )(*moved)
    return w1_new, h1_new, w2t_new.T, h2_new


def solution(mesh):
    placed = (P("gene", "cell"), P(("gene", "cell"), None), P(None, "cell"), P(), P(None, "cell"))
    return jax.shard_map(
        on_device,
        mesh=mesh,
        in_specs=placed,
        out_specs=(P(("gene", "cell"), None), P(None, "cell"), P(), P(None, "cell")),
        check_vma=False,
    )
```

```python
import jax
import jax.numpy as jnp
from jax import lax
from jax.experimental import pallas as pl
from jax.experimental.pallas import tpu as pltpu
from jax.sharding import PartitionSpec as P

NX, NY, NZ, NC = 4, 4, 2, 2
NG = 4
F32, BF16, I16 = jnp.float32, jnp.bfloat16, jnp.int16
HI = lax.Precision.HIGHEST
TOP = 32767.0
ORDER = (1, 3, 2)

SIZES = dict(
    z=1, a2=12, a3=18, f=8, m=3, nd=4, n=8, hb=4, hf=4, hs=6, h2=3, e1=8, p=6, ps=6, q=6, qs=6, l=1, ls=1,
    s0=1, s1=3, s2=1, s3=3, s4=3, s5=3, s6=1,
)
PLACE, S_ALL = {}, 0
for _name, _size in SIZES.items():
    PLACE[_name] = S_ALL
    S_ALL += _size


def nt(a, b, precision=None):
    return lax.dot_general(
        a, b, (((1,), (1,)), ((), ())), preferred_element_type=F32, precision=precision
    )


def high(a, b):
    return jnp.dot(a, b, precision=HI, preferred_element_type=F32)


def most_of(v, axis):
    return jnp.maximum(jnp.max(v, axis=axis, keepdims=True), 1e-30)


def coded(v, most):
    return jnp.round(v * (TOP / most)).astype(jnp.int32).astype(I16)


def decoded(q, most):
    return q.astype(jnp.int32).astype(F32) * (most * (1.0 / TOP))


def kernel(
    counts, w1, h1, w2t, h2,
    w1_out, h1_out, w2t_out, h2_out,
    wg, cnt, h1v, w2tv, h2v, hl, num, nq, nqr, nm, nmr, cs, fr, hq, hs, h1f, h2b,
    rb, e1r, acc, pq, pqr, ps, psr, aq, aqr, aps, apr, fin, lq, lqr, lps, lpr,
    sm, smr, sv, svr, sz, szr, sx, sy, sg, w1f, w2f,
    snd, rcv, loc,
):
    g = lax.axis_index("gene")
    ci = lax.axis_index("cell")
    mx, my, mz, mc = ci // 16, (ci // 4) % 4, (ci // 2) % 2, ci % 2
    oz, oc = 1 - mz, 1 - mc

    def cell(x, y, z, c):
        return ((x * NY + y) * NZ + z) * NC + c

    def at_x(d):
        return (mx + d) % NX

    def at_y(d):
        return (my + d) % NY

    def at_g(d):
        return (g + d) % NG

    def copy(src, dst, name, k, to):
        sem = PLACE[name] + k
        return pltpu.make_async_remote_copy(
            src_ref=src,
            dst_ref=dst,
            send_sem=snd.at[sem],
            recv_sem=rcv.at[sem],
            device_id=to,
            device_id_type=pl.DeviceIdType.MESH,
        )

    sibling = (g, cell(mx, my, mz, oc))
    z_pair = (g, cell(mx, my, oz, mc))

    def to_x(d):
        return (g, cell(at_x(d), my, mz, mc))

    def to_y(d):
        return (g, cell(mx, at_y(d), mz, mc))

    def to_g(d):
        return (at_g(d), ci)

    own = wg.at[mx, my, mz, mc]
    barrier = pltpu.get_barrier_semaphore()
    partners = [sibling, z_pair]
    for d in range(1, 4):
        partners += [to_x(d), to_y(d), to_g(d)]
    for to in partners:
        pl.semaphore_signal(barrier, inc=1, device_id=to, device_id_type=pl.DeviceIdType.MESH)
    read_w1 = pltpu.make_async_copy(w1, own, loc.at[0])
    read_h1 = pltpu.make_async_copy(h1, h1v, loc.at[1])
    read_w2 = pltpu.make_async_copy(w2t, w2tv, loc.at[2])
    read_h2 = pltpu.make_async_copy(h2, h2v, loc.at[3])
    read_counts = pltpu.make_async_copy(counts, cnt, loc.at[4])
    for read in (read_w1, read_h1, read_w2, read_h2, read_counts):
        read.start()
    read_w1.wait()
    pl.semaphore_wait(barrier, len(partners))

    go_z = copy(own, own, "z", 0, z_pair)
    go_z.start()

    def near(k, a, d):
        src = wg.at[mx, my, oz if k else mz, mc]
        return copy(src, src, "a2", 6 * k + 3 * a + d - 1, to_y(d) if a else to_x(d))

    for d in ORDER:
        for a in range(2):
            near(0, a, d).start()
    read_h1.wait()
    hl[...] = h1v[...].astype(BF16)
    num[...] = jnp.zeros_like(num)
    cs[...] = jnp.zeros_like(cs)
    go_z.wait_recv()
    for d in ORDER:
        for a in range(2):
            near(1, a, d).start()

    def column(h, d):
        return wg.at[:, at_y(4 - d), :, mc, 0] if h == 0 else wg.at[at_x(4 - d), :, :, mc, 1]

    def far(h, e, d):
        src = wg.at[mx, at_y(4 - e), :, mc, 1] if h else wg.at[at_x(4 - e), my, :, mc, 0]
        return copy(src, src, "a3", 9 * h + 3 * (e - 1) + d - 1, to_x(d) if h else to_y(d))

    def forward(h, d):
        src = column(h, d)
        return copy(src, src, "f", 4 * h + d, sibling)

    for e in ORDER:
        for h in range(2):
            near(0, h, e).wait_recv()
            near(1, h, e).wait_recv()
            for d in ORDER:
                far(h, e, d).start()
    for h in range(2):
        forward(h, 0).start()

    read_counts.wait()

    def pass_on(d):
        for h in range(2):
            for e in ORDER:
                far(h, e, d).wait_recv()
            forward(h, d).start()

    def first(w, v):
        approx = jnp.dot(w, hl[...], preferred_element_type=F32)
        ratio = (v.astype(F32) / approx).astype(BF16)
        add = lax.dot_general(
            w, ratio, (((0,), (0,)), ((), ())), preferred_element_type=F32
        )
        for j in range(NG):
            num[j] += add[:, j * 128 : (j + 1) * 128]
        cs[...] += jnp.sum(w.astype(F32).reshape(-1, 8, w.shape[1]), axis=0)

    def first_step(t, carry):
        d = t + t // 2 - 2 * (t // 3)
        forward(0, d).wait_recv()
        first(
            wg[:, at_y(4 - d), :, :, 0].reshape(512, 512),
            cnt[:, at_y(4 - d), :, :, 0].reshape(512, 512),
        )
        forward(1, d).wait_recv()
        first(
            wg[at_x(4 - d), :, :, :, 1].reshape(512, 512),
            cnt[at_x(4 - d), :, :, :, 1].reshape(512, 512),
        )

        @pl.when(t == 0)
        def _():
            pass_on(1)
            pass_on(3)

        @pl.when(t == 1)
        def _():
            pass_on(2)

        return carry

    lax.fori_loop(0, 4, first_step, 0)

    def rows(b, p):
        return slice(256 * b + 128 * p, 256 * b + 128 * p + 128)

    def send_marks(d):
        return copy(nm.at[d - 1], nmr.at[d - 1], "m", d - 1, to_g(d))

    def send_diag(b, p):
        at = rows(b, p)
        return copy(nq.at[1, at], nqr.at[1, at], "nd", 2 * b + p, to_g(3 if p else 1))

    def send_num(b, d, p):
        at = rows(b, p)
        return copy(nq.at[d - 1, at], nqr.at[d - 1, at], "n", 4 * b + 2 * p + d // 3, to_g(d))

    def send_h(b, d):
        return copy(hq.at[b, g], hq.at[b, g], "hb", 2 * b + d // 3, to_g(d))

    def send_hs(b, d):
        return copy(hs.at[b, g], hs.at[b, g], "hs", 3 * b + d - 1, to_g(d))

    def pass_h(b, p):
        src = hq.at[b, at_g(1 if p else 3), 128 * p : 128 * p + 128]
        return copy(src, src, "hf", 2 * b + p, to_g(3 if p else 1))

    far_most = most_of(num[at_g(2)], 0)
    for d in (2, 1, 3):
        most = far_most if d == 2 else most_of(num[at_g(d)], 0)
        nm[d - 1, :, 0:512] = cs[...]
        nm[d - 1, :, 512:640] = jnp.broadcast_to(most, (8, 128))
        nm[d - 1, :, 640:768] = jnp.broadcast_to(far_most, (8, 128))
        send_marks(d).start()

    def code_num(b, d, p, more, most):
        at = rows(b, p)
        value = num[at_g(d), at]
        if more is not None:
            value += decoded(nqr[1, at], more)
        nq[d - 1, at] = coded(value, most)

    def mark(d):
        return nm[d - 1, 0:1, 512:640]

    def sent_mark(d, k=0):
        return nmr[d - 1, 0:1, 512 + 128 * k : 640 + 128 * k]

    for b in range(2):
        for p in range(2):
            code_num(b, 2, p, None, far_most)
            send_diag(b, p).start()
        for d, p in ((1, 1), (3, 0)):
            code_num(b, d, p, None, mark(d))
            send_num(b, d, p).start()
    read_w2.wait()
    read_h2.wait()
    w2 = jnp.transpose(w2tv[...])
    mine = pl.ds(pl.multiple_of(g * 128, 128), 128)
    h2_mine = h2v[:, mine]
    fit = high(w2, h2_mine)
    for d in ORDER:
        send_marks(d).wait_recv()
    for b in range(2):
        for d, p in ((1, 0), (3, 1)):
            send_diag(b, p).wait_recv()
            code_num(b, d, p, sent_mark(d, 1), mark(d) + sent_mark(d, 1))
            send_num(b, d, p).start()
    parts = cs[...] + nmr[0, :, 0:512] + nmr[1, :, 0:512] + nmr[2, :, 0:512]
    total = jnp.sum(parts, axis=0, keepdims=True)
    colsum = jnp.transpose(jnp.broadcast_to(total, (128, 512)))
    for b in range(2):
        for p in range(2):
            at = rows(b, p)
            h1_num = num[g, at]
            for d in (3, 1) if p == 0 else (1, 3):
                send_num(b, d, p).wait_recv()
                joined = (d == 1) == (p == 0)
                most = sent_mark(d) + sent_mark(2) if joined else sent_mark(d)
                h1_num += decoded(nqr[d - 1, at], most)
            fr[at] = h1v[at, mine] * h1_num / colsum[at]
        new = fr[256 * b : 256 * b + 256]
        most = most_of(new, 0)
        hq[b, g] = coded(new, most)
        hs[b, g] = jnp.broadcast_to(most, (8, 128))
        for d in (1, 3):
            send_h(b, d).start()
        for d in ORDER:
            send_hs(b, d).start()

    def take_h(b, d):
        j = at_g(4 - d)
        value = decoded(hq[b, j], hs[b, j, 0:1])
        there = pl.ds(pl.multiple_of(j * 128, 128), 128)
        here = pl.ds(256 * b, 256)
        h1f[here, there] = value
        hl[here, there] = value.astype(BF16)

    def take_near(b):
        for d in (1, 3):
            send_h(b, d).wait_recv()
            pass_h(b, d // 3).start()
        take_h(b, 0)
        for d in (1, 3):
            send_hs(b, d).wait_recv()
            take_h(b, d)

    def take_far(b):
        send_hs(b, 2).wait_recv()
        for p in range(2):
            pass_h(b, p).wait_recv()
        take_h(b, 2)

    take_near(0)
    fresh = fr[...]

    ratio3 = fresh / fit
    lift = high(w2tv[...], ratio3)
    h2_new = h2_mine * lift / jnp.sum(w2tv[...], axis=1, keepdims=True)
    h2b[g] = h2_new
    ratio4 = fresh / high(w2, h2_new)
    w2_part = nt(h2_new, ratio4, HI)
    h2_part = jnp.broadcast_to(jnp.sum(h2_new, axis=1, keepdims=True), (64, 128))
    h1_rows = nt(jnp.ones((8, 128), F32), fresh, HI)
    for j in range(NG):
        for c in range(NC):
            at = 16 * j + 8 * c
            sm[c, j, :, 0:512] = w2_part[at : at + 8]
            sm[c, j, :, 512:640] = h2_part[at : at + 8]
            sm[c, j, :, 640:768] = jnp.zeros((8, 128), F32)
            for k in range(4):
                sm[c, j, k : k + 1, 640:768] = h1_rows[0:1, k * 128 : (k + 1) * 128]

    sum_c = copy(sm.at[oc], smr, "s0", 0, sibling)

    def sum_g(d):
        return copy(sv.at[at_g(d)], svr.at[d - 1], "s1", d - 1, to_g(d))

    sum_z = copy(sz, szr, "s2", 0, z_pair)

    def sum_x(d):
        return copy(sx.at[mx], sx.at[mx], "s3", d - 1, to_x(d))

    def sum_y(d):
        return copy(sy.at[my], sy.at[my], "s4", d - 1, to_y(d))

    def all_g(d):
        return copy(sg.at[mc, g], sg.at[mc, g], "s5", d - 1, to_g(d))

    all_c = copy(sg.at[mc], sg.at[mc], "s6", 0, sibling)

    def send_h2(d):
        return copy(h2b.at[g], h2b.at[g], "h2", d - 1, to_g(d))

    sum_c.start()
    take_near(1)
    sum_c.wait_recv()
    sv[...] = sm[mc] + smr[...]
    for d in ORDER:
        sum_g(d).start()
    take_far(0)
    take_far(1)

    def second(h, i):
        d = i + 1
        w = wg[:, at_y(d), :, :, 1] if h else wg[at_x(d), :, :, :, 0]
        v = cnt[:, at_y(d), :, :, 1] if h else cnt[at_x(d), :, :, :, 0]
        approx = jnp.dot(w.reshape(512, 512), hl[...], preferred_element_type=F32)
        ratio = (v.reshape(512, 512).astype(F32) / approx).astype(BF16)
        rb[h, i] = nt(ratio, hl[...]).reshape(4, 2, 2, 32, 512)

    def to_sibling(h, i):
        return copy(rb.at[h, i, :, :, oc], e1r.at[h, i], "e1", 4 * h + i, sibling)

    def along(h, i):
        to = to_x(i + 1) if h == 0 else to_y(i + 1)
        return (
            copy(pq.at[h, i], pqr.at[h, i], "p", 3 * h + i, to),
            copy(ps.at[h, i], psr.at[h, i], "ps", 3 * h + i, to),
        )

    def add_up(h, i):
        to_sibling(h, i).wait_recv()
        both = rb[h, i, :, :, mc] + e1r[h, i]

        @pl.when(i < 3)
        def _():
            v = both.reshape(8, 32, 512)
            most = most_of(v, 1)
            pq[h, i] = coded(v, most).reshape(4, 2, 32, 512)
            ps[h, i] = most.reshape(8, 512)
            for go in along(h, i):
                go.start()

        @pl.when(i == 3)
        def _():
            acc[h] = both

    def second_step(i, carry):
        @pl.when(i < 4)
        def _():
            for h in range(2):
                second(h, i)
                to_sibling(h, i).start()

        @pl.when(i > 0)
        def _():
            for h in range(2):
                add_up(h, i - 1)

        @pl.when(i == 1)
        def _():
            for d in ORDER:
                sum_g(d).wait_recv()
            sz[...] = sv[g] + svr[0] + svr[1] + svr[2]
            sum_z.start()
            for d in ORDER:
                send_h2(d).start()

        @pl.when(i == 2)
        def _():
            sum_z.wait_recv()
            sx[mx] = sz[...] + szr[...]
            for d in ORDER:
                sum_x(d).start()

        @pl.when(i == 4)
        def _():
            for d in ORDER:
                sum_x(d).wait_recv()
            sy[my] = sx[0] + sx[1] + sx[2] + sx[3]
            for d in ORDER:
                sum_y(d).start()

        return carry

    lax.fori_loop(0, 5, second_step, 0)
    put_h1 = pltpu.make_async_copy(h1f, h1_out, loc.at[5])
    put_h1.start()

    def across(h, d):
        to = to_y(d) if h == 0 else to_x(d)
        k = 3 * h + d - 1
        return (
            copy(aq.at[h, d - 1], aqr.at[h, d - 1], "q", k, to),
            copy(aps.at[h, d - 1], apr.at[h, d - 1], "qs", k, to),
        )

    for i in range(3):
        if i == 1:
            for d in ORDER:
                sum_y(d).wait_recv()
            done = sy[0] + sy[1] + sy[2] + sy[3]
            sg[mc, g] = done
            for d in ORDER:
                all_g(d).start()
        for h in range(2):
            for go in along(h, i):
                go.wait_recv()
            more = decoded(pqr[h, i].reshape(8, 32, 512), psr[h, i].reshape(8, 1, 512))
            acc[h] += more.reshape(4, 2, 32, 512)
            if i == 2:
                for d in ORDER:
                    v = acc[h, at_y(d) if h == 0 else at_x(d)]
                    most = most_of(v, 1)
                    aq[h, d - 1] = coded(v, most)
                    aps[h, d - 1] = jnp.broadcast_to(most, (2, 8, 512))
                    for go in across(h, d):
                        go.start()
    for d in ORDER:
        all_g(d).wait_recv()
    all_c.start()
    for d in ORDER:
        send_h2(d).wait_recv()
    puts = [
        pltpu.make_async_copy(h2b.at[j], h2_out.at[:, 128 * j : 128 * j + 128], loc.at[6 + j])
        for j in range(NG)
    ]
    for put in puts:
        put.start()
    rowsum = jnp.concatenate([done[k : k + 1, 640:768] for k in range(4)], axis=1)
    for h in range(2):
        whole = acc[h, my if h == 0 else mx]
        for d in ORDER:
            for go in across(h, d):
                go.wait_recv()
            whole += decoded(aqr[h, d - 1], apr[h, d - 1, :, 0:1])
        fin[:, h] = whole
    most = most_of(fin[oz], 1)
    lq[...] = coded(fin[oz], most)
    lps[...] = jnp.broadcast_to(most, (2, 8, 512))
    last = (copy(lq, lqr, "l", 0, z_pair), copy(lps, lpr, "ls", 0, z_pair))
    for go in last:
        go.start()
    all_c.wait_recv()
    for j in range(NG):
        for c in range(NC):
            at = slice(16 * j + 8 * c, 16 * j + 8 * c + 8)
            w2f[at, :] = w2tv[at, :] * sg[c, j, :, 0:512] / sg[c, j, :, 512:513]
    puts.append(pltpu.make_async_copy(w2f, w2t_out, loc.at[11]))
    puts[-1].start()
    for go in last:
        go.wait_recv()
    w1_num = (fin[mz] + decoded(lqr[...], lpr[:, 0:1])).reshape(64, 512)
    w1_now = wg[mx, my, mz, mc].astype(F32).reshape(64, 512)
    w1f[...] = (w1_now * w1_num / rowsum).astype(BF16)
    puts.append(pltpu.make_async_copy(w1f, w1_out, loc.at[10]))
    puts[-1].start()

    for sent in (go_z, sum_c, sum_z, all_c) + last:
        sent.wait_send()
    for d in ORDER:
        for h in range(2):
            for sent in (near(0, h, d), near(1, h, d), send_hs(h, d)):
                sent.wait_send()
            for e in ORDER:
                far(h, e, d).wait_send()
            for sent in along(h, d - 1) + across(h, d):
                sent.wait_send()
        for sent in (send_marks, send_h2, sum_g, sum_x, sum_y, all_g):
            sent(d).wait_send()
    for b in range(2):
        for p in range(2):
            for sent in (send_diag(b, p), pass_h(b, p), send_h(b, 3 if p else 1)):
                sent.wait_send()
            for d in (1, 3):
                send_num(b, d, p).wait_send()
    for h in range(2):
        for d in range(4):
            forward(h, d).wait_send()
            to_sibling(h, d).wait_send()
    for put in puts + [put_h1]:
        put.wait()


def finish(w1, h1, w2t, h2, w1_out, h1_out, w2t_out, h2_out, w1v, h1v, w2tv, h2v, sem):
    rows = [pl.ds(128 * k, 128) for k in range(4)]
    steps = [(h1.at[r], h1v.at[r], h1_out.at[r]) for r in rows]
    steps += [(w1, w1v, w1_out), (w2t, w2tv, w2t_out), (h2, h2v, h2_out)]
    loads = [pltpu.make_async_copy(a, v, sem.at[0, k]) for k, (a, v, o) in enumerate(steps)]
    stores = [pltpu.make_async_copy(v, o, sem.at[1, k]) for k, (a, v, o) in enumerate(steps)]
    for go in loads:
        go.start()
    for load, store in zip(loads, stores):
        load.wait()
        store.start()
    for go in stores:
        go.wait()


def on_device(counts, w1, h1, w2, h2):
    anywhere = pl.BlockSpec(memory_space=pl.ANY)
    shape = (NX, NY, NZ, NC, 2, 32, 512)
    sds = jax.ShapeDtypeStruct
    outs = (
        sds((64, 512), BF16),
        sds((512, 512), F32),
        sds((64, 512), F32),
        sds((64, 512), F32),
    )
    scratch = [
        (shape, BF16), (shape, jnp.int32), ((512, 512), F32), ((64, 512), F32), ((64, 512), F32),
        ((512, 512), BF16), ((NG, 512, 128), F32), ((3, 512, 128), I16), ((3, 512, 128), I16),
        ((3, 8, 768), F32), ((3, 8, 768), F32), ((8, 512), F32),
        ((512, 128), F32), ((2, NG, 256, 128), I16), ((2, NG, 8, 128), F32), ((512, 512), F32), ((NG, 64, 128), F32),
        ((2, 4, 4, 2, 2, 32, 512), F32), ((2, 4, 4, 2, 32, 512), F32), ((2, 4, 2, 32, 512), F32),
        ((2, 3, 4, 2, 32, 512), I16), ((2, 3, 4, 2, 32, 512), I16), ((2, 3, 8, 512), F32), ((2, 3, 8, 512), F32),
        ((2, 3, 2, 32, 512), I16), ((2, 3, 2, 32, 512), I16), ((2, 3, 2, 8, 512), F32), ((2, 3, 2, 8, 512), F32),
        ((2, 2, 32, 512), F32), ((2, 32, 512), I16), ((2, 32, 512), I16), ((2, 8, 512), F32), ((2, 8, 512), F32),
        ((2, NG, 8, 768), F32), ((NG, 8, 768), F32), ((NG, 8, 768), F32), ((3, 8, 768), F32), ((8, 768), F32),
        ((8, 768), F32), ((4, 8, 768), F32), ((4, 8, 768), F32), ((2, NG, 8, 768), F32),
        ((64, 512), BF16), ((64, 512), F32),
    ]
    moved = pl.pallas_call(
        kernel,
        out_shape=outs,
        in_specs=[anywhere] * 5,
        out_specs=(anywhere,) * 4,
        scratch_shapes=[pltpu.VMEM(*s) for s in scratch]
        + [
            pltpu.SemaphoreType.DMA((S_ALL,)),
            pltpu.SemaphoreType.DMA((S_ALL,)),
            pltpu.SemaphoreType.DMA((12,)),
        ],
        compiler_params=pltpu.CompilerParams(
            collective_id=0, has_side_effects=True, vmem_limit_bytes=56 * 1024 * 1024
        ),
    )(counts.reshape(shape), w1.reshape(2, 32, 512), h1, w2.T, h2)
    w1_new, h1_new, w2t_new, h2_new = pl.pallas_call(
        finish,
        out_shape=outs,
        in_specs=[anywhere] * 4,
        out_specs=(anywhere,) * 4,
        scratch_shapes=[pltpu.VMEM(o.shape, o.dtype) for o in outs]
        + [pltpu.SemaphoreType.DMA((2, 7))],
    )(*moved)
    return w1_new, h1_new, w2t_new.T, h2_new


def solution(mesh):
    placed = (P("gene", "cell"), P(("gene", "cell"), None), P(None, "cell"), P(), P(None, "cell"))
    return jax.shard_map(
        on_device,
        mesh=mesh,
        in_specs=placed,
        out_specs=(P(("gene", "cell"), None), P(None, "cell"), P(), P(None, "cell")),
        check_vma=False,
    )
```

```python
import jax
import jax.numpy as jnp
from jax import lax
from jax.experimental import pallas as pl
from jax.experimental.pallas import tpu as pltpu
from jax.sharding import PartitionSpec as P

NX, NY, NZ, NC = 4, 4, 2, 2
NG = 4
F32, BF16, I16 = jnp.float32, jnp.bfloat16, jnp.int16
HI = lax.Precision.HIGHEST
TOP = 32767.0
ORDER = (1, 3, 2)

SIZES = dict(
    z=1, a2=12, a3=36, f=8, m=3, nd=4, n=8, hb=4, hf=4, hs=6, h2=3, e1=8, p=6, ps=6, q=6, qs=6, l=1, ls=1,
    s0=1, s1=3, s2=3, s3=1, s4=3, s5=3, s6=1,
)
PLACE, S_ALL = {}, 0
for _name, _size in SIZES.items():
    PLACE[_name] = S_ALL
    S_ALL += _size


def nt(a, b, precision=None):
    return lax.dot_general(
        a, b, (((1,), (1,)), ((), ())), preferred_element_type=F32, precision=precision
    )


def high(a, b):
    return jnp.dot(a, b, precision=HI, preferred_element_type=F32)


def most_of(v, axis):
    return jnp.maximum(jnp.max(v, axis=axis, keepdims=True), 1e-30)


def coded(v, most):
    return jnp.round(v * (TOP / most)).astype(jnp.int32).astype(I16)


def decoded(q, most):
    return q.astype(jnp.int32).astype(F32) * (most * (1.0 / TOP))


def kernel(
    counts, w1, h1, w2t, h2,
    w1_out, h1_out, w2t_out, h2_out,
    wg, cnt, h1v, w2tv, h2v, hl, num, nq, nqr, nm, nmr, cs, fr, hq, hs, h2b,
    rb, e1r, acc, pq, pqr, ps, psr, aq, aqr, aps, apr, fin, lq, lqr, lps, lpr,
    sm, smr, sv, svr, sz, szr, sx, sy, sg,
    snd, rcv, loc,
):
    g = lax.axis_index("gene")
    ci = lax.axis_index("cell")
    mx, my, mz, mc = ci // 16, (ci // 4) % 4, (ci // 2) % 2, ci % 2
    oz, oc = 1 - mz, 1 - mc

    def cell(x, y, z, c):
        return ((x * NY + y) * NZ + z) * NC + c

    def at_x(d):
        return (mx + d) % NX

    def at_y(d):
        return (my + d) % NY

    def at_g(d):
        return (g + d) % NG

    def copy(src, dst, name, k, to):
        sem = PLACE[name] + k
        return pltpu.make_async_remote_copy(
            src_ref=src,
            dst_ref=dst,
            send_sem=snd.at[sem],
            recv_sem=rcv.at[sem],
            device_id=to,
            device_id_type=pl.DeviceIdType.MESH,
        )

    sibling = (g, cell(mx, my, mz, oc))
    z_pair = (g, cell(mx, my, oz, mc))

    def to_x(d):
        return (g, cell(at_x(d), my, mz, mc))

    def to_y(d):
        return (g, cell(mx, at_y(d), mz, mc))

    def to_g(d):
        return (at_g(d), ci)

    own = wg.at[mx, my, mz, mc]
    barrier = pltpu.get_barrier_semaphore()
    partners = [sibling, z_pair]
    for d in range(1, 4):
        partners += [to_x(d), to_y(d), to_g(d)]
    for to in partners:
        pl.semaphore_signal(barrier, inc=1, device_id=to, device_id_type=pl.DeviceIdType.MESH)
    read_w1 = pltpu.make_async_copy(w1, own, loc.at[0])
    read_h1 = pltpu.make_async_copy(h1, h1v, loc.at[1])
    read_w2 = pltpu.make_async_copy(w2t, w2tv, loc.at[2])
    read_h2 = pltpu.make_async_copy(h2, h2v, loc.at[3])
    read_counts = pltpu.make_async_copy(counts, cnt, loc.at[4])
    for read in (read_w1, read_h1, read_w2, read_h2, read_counts):
        read.start()
    read_w1.wait()
    pl.semaphore_wait(barrier, len(partners))

    go_z = copy(own, own, "z", 0, z_pair)
    go_z.start()

    def near(k, a, d):
        src = wg.at[mx, my, oz if k else mz, mc]
        return copy(src, src, "a2", 6 * k + 3 * a + d - 1, to_y(d) if a else to_x(d))

    for d in ORDER:
        for a in range(2):
            near(0, a, d).start()
    read_h1.wait()
    hl[...] = h1v[...].astype(BF16)
    num[...] = jnp.zeros_like(num)
    cs[...] = jnp.zeros_like(cs)
    go_z.wait_recv()
    for d in ORDER:
        for a in range(2):
            near(1, a, d).start()

    def column(h, d):
        return wg.at[:, at_y(4 - d), :, mc, 0] if h == 0 else wg.at[at_x(4 - d), :, :, mc, 1]

    def far(k, h, e, d):
        z = oz if k else mz
        src = wg.at[mx, at_y(4 - e), z, mc, 1] if h else wg.at[at_x(4 - e), my, z, mc, 0]
        to = to_x(d) if h else to_y(d)
        return copy(src, src, "a3", 18 * k + 9 * h + 3 * (e - 1) + d - 1, to)

    def forward(h, d):
        src = column(h, d)
        return copy(src, src, "f", 4 * h + d, sibling)

    for k in range(2):
        for e in ORDER:
            for h in range(2):
                near(k, h, e).wait_recv()
                for d in (1, 3):
                    far(k, h, e, d).start()
    for k in range(2):
        for e in ORDER:
            for h in range(2):
                far(k, h, e, 2).start()
    for h in range(2):
        forward(h, 0).start()

    read_counts.wait()

    def pass_on(d):
        for h in range(2):
            for e in ORDER:
                far(0, h, e, d).wait_recv()
                far(1, h, e, d).wait_recv()
            forward(h, d).start()

    def first(w, v):
        approx = jnp.dot(w, hl[...], preferred_element_type=F32)
        ratio = (v.astype(F32) / approx).astype(BF16)
        add = lax.dot_general(
            w, ratio, (((0,), (0,)), ((), ())), preferred_element_type=F32
        )
        for j in range(NG):
            num[j] += add[:, j * 128 : (j + 1) * 128]
        cs[...] += jnp.sum(w.astype(F32).reshape(-1, 8, w.shape[1]), axis=0)

    def first_step(t, carry):
        d = t + t // 2 - 2 * (t // 3)
        forward(0, d).wait_recv()
        first(
            wg[:, at_y(4 - d), :, :, 0].reshape(512, 512),
            cnt[:, at_y(4 - d), :, :, 0].reshape(512, 512),
        )
        forward(1, d).wait_recv()
        first(
            wg[at_x(4 - d), :, :, :, 1].reshape(512, 512),
            cnt[at_x(4 - d), :, :, :, 1].reshape(512, 512),
        )

        @pl.when(t == 0)
        def _():
            pass_on(1)
            pass_on(3)

        @pl.when(t == 1)
        def _():
            pass_on(2)

        return carry

    lax.fori_loop(0, 4, first_step, 0)

    def rows(b, p):
        return slice(256 * b + 128 * p, 256 * b + 128 * p + 128)

    def send_marks(d):
        return copy(nm.at[d - 1], nmr.at[d - 1], "m", d - 1, to_g(d))

    def send_diag(b, p):
        at = rows(b, p)
        return copy(nq.at[1, at], nqr.at[1, at], "nd", 2 * b + p, to_g(3 if p else 1))

    def send_num(b, d, p):
        at = rows(b, p)
        return copy(nq.at[d - 1, at], nqr.at[d - 1, at], "n", 4 * b + 2 * p + d // 3, to_g(d))

    def send_h(b, d):
        return copy(hq.at[b, g], hq.at[b, g], "hb", 2 * b + d // 3, to_g(d))

    def send_hs(b, d):
        return copy(hs.at[b, g], hs.at[b, g], "hs", 3 * b + d - 1, to_g(d))

    def pass_h(b, p):
        src = hq.at[b, at_g(1 if p else 3), 128 * p : 128 * p + 128]
        return copy(src, src, "hf", 2 * b + p, to_g(3 if p else 1))

    far_most = most_of(num[at_g(2)], 0)
    for d in (2, 1, 3):
        most = far_most if d == 2 else most_of(num[at_g(d)], 0)
        nm[d - 1, :, 0:512] = cs[...]
        nm[d - 1, :, 512:640] = jnp.broadcast_to(most, (8, 128))
        nm[d - 1, :, 640:768] = jnp.broadcast_to(far_most, (8, 128))
        send_marks(d).start()

    def code_num(b, d, p, more, most):
        at = rows(b, p)
        value = num[at_g(d), at]
        if more is not None:
            value += decoded(nqr[1, at], more)
        nq[d - 1, at] = coded(value, most)

    def mark(d):
        return nm[d - 1, 0:1, 512:640]

    def sent_mark(d, k=0):
        return nmr[d - 1, 0:1, 512 + 128 * k : 640 + 128 * k]

    def start_diag(b):
        for p in range(2):
            code_num(b, 2, p, None, far_most)
            send_diag(b, p).start()

    def start_own(b):
        for d, p in ((1, 1), (3, 0)):
            code_num(b, d, p, None, mark(d))
            send_num(b, d, p).start()

    def start_joined(b):
        for d, p in ((1, 0), (3, 1)):
            send_diag(b, p).wait_recv()
            code_num(b, d, p, sent_mark(d, 1), mark(d) + sent_mark(d, 1))
            send_num(b, d, p).start()

    start_diag(0)
    start_own(0)
    start_diag(1)
    read_w2.wait()
    read_h2.wait()
    w2 = jnp.transpose(w2tv[...])
    mine = pl.ds(pl.multiple_of(g * 128, 128), 128)
    h2_mine = h2v[:, mine]
    fit = high(w2, h2_mine)
    for d in ORDER:
        send_marks(d).wait_recv()
    start_joined(0)
    start_own(1)
    start_joined(1)
    parts = cs[...] + nmr[0, :, 0:512] + nmr[1, :, 0:512] + nmr[2, :, 0:512]
    total = jnp.sum(parts, axis=0, keepdims=True)
    colsum = jnp.transpose(jnp.broadcast_to(total, (128, 512)))
    for b in range(2):
        for p in range(2):
            at = rows(b, p)
            h1_num = num[g, at]
            for d in (3, 1) if p == 0 else (1, 3):
                send_num(b, d, p).wait_recv()
                joined = (d == 1) == (p == 0)
                most = sent_mark(d) + sent_mark(2) if joined else sent_mark(d)
                h1_num += decoded(nqr[d - 1, at], most)
            fr[at] = h1v[at, mine] * h1_num / colsum[at]
        new = fr[256 * b : 256 * b + 256]
        most = most_of(new, 0)
        hq[b, g] = coded(new, most)
        hs[b, g] = jnp.broadcast_to(most, (8, 128))
        for d in (1, 3):
            send_h(b, d).start()
        for d in ORDER:
            send_hs(b, d).start()

    def take_h(b, d):
        j = at_g(4 - d)
        value = decoded(hq[b, j], hs[b, j, 0:1])
        there = pl.ds(pl.multiple_of(j * 128, 128), 128)
        here = pl.ds(256 * b, 256)
        h1_out[here, there] = value
        hl[here, there] = value.astype(BF16)

    def take_near(b):
        for d in (1, 3):
            send_h(b, d).wait_recv()
            pass_h(b, d // 3).start()
        take_h(b, 0)
        for d in (1, 3):
            send_hs(b, d).wait_recv()
            take_h(b, d)

    def take_far(b):
        send_hs(b, 2).wait_recv()
        for p in range(2):
            pass_h(b, p).wait_recv()
        take_h(b, 2)

    fresh = fr[...]

    ratio3 = fresh / fit
    lift = high(w2tv[...], ratio3)
    h2_new = h2_mine * lift / jnp.sum(w2tv[...], axis=1, keepdims=True)
    h2b[g] = h2_new
    ratio4 = fresh / high(w2, h2_new)
    w2_part = nt(h2_new, ratio4, HI)
    h2_part = jnp.broadcast_to(jnp.sum(h2_new, axis=1, keepdims=True), (64, 128))
    h1_rows = nt(jnp.ones((8, 128), F32), fresh, HI)
    for j in range(NG):
        for c in range(NC):
            at = 16 * j + 8 * c
            sm[c, j, :, 0:512] = w2_part[at : at + 8]
            sm[c, j, :, 512:640] = h2_part[at : at + 8]
            sm[c, j, :, 640:768] = jnp.zeros((8, 128), F32)
            for k in range(4):
                sm[c, j, k : k + 1, 640:768] = h1_rows[0:1, k * 128 : (k + 1) * 128]

    sum_c = copy(sm.at[oc], smr, "s0", 0, sibling)

    def sum_x(d):
        return copy(sv.at[at_x(d)], svr.at[d - 1], "s1", d - 1, to_x(d))

    def sum_y(d):
        return copy(sy.at[my], sy.at[my], "s2", d - 1, to_y(d))

    sum_z = copy(sz, szr, "s3", 0, z_pair)

    def sum_g(d):
        return copy(sx.at[g], sx.at[g], "s4", d - 1, to_g(d))

    def all_x(d):
        return copy(sg.at[mc, mx], sg.at[mc, mx], "s5", d - 1, to_x(d))

    all_c = copy(sg.at[mc], sg.at[mc], "s6", 0, sibling)

    def send_h2(d):
        return copy(h2b.at[g], h2b.at[g], "h2", d - 1, to_g(d))

    sum_c.start()
    take_near(0)
    sum_c.wait_recv()
    sv[...] = sm[mc] + smr[...]
    for d in ORDER:
        sum_x(d).start()
    take_near(1)
    for d in ORDER:
        sum_x(d).wait_recv()
    sy[my] = sv[mx] + svr[0] + svr[1] + svr[2]
    for d in ORDER:
        sum_y(d).start()
    take_far(0)
    take_far(1)
    for d in ORDER:
        sum_y(d).wait_recv()
    sz[...] = sy[0] + sy[1] + sy[2] + sy[3]
    sum_z.start()

    def place(i):
        return (i + 2 + i // 2 + 2 * (i // 3)) % 4

    def second(h, i):
        d = place(i)
        w = wg[:, at_y(d), :, :, 1] if h else wg[at_x(d), :, :, :, 0]
        v = cnt[:, at_y(d), :, :, 1] if h else cnt[at_x(d), :, :, :, 0]
        approx = jnp.dot(w.reshape(512, 512), hl[...], preferred_element_type=F32)
        ratio = (v.reshape(512, 512).astype(F32) / approx).astype(BF16)
        rb[h, i] = nt(ratio, hl[...]).reshape(4, 2, 2, 32, 512)

    def to_sibling(h, i):
        return copy(rb.at[h, i, :, :, oc], e1r.at[h, i], "e1", 4 * h + i, sibling)

    def along(h, i):
        to = to_x(place(i)) if h == 0 else to_y(place(i))
        return (
            copy(pq.at[h, i], pqr.at[h, i], "p", 3 * h + i, to),
            copy(ps.at[h, i], psr.at[h, i], "ps", 3 * h + i, to),
        )

    def add_up(h, i):
        to_sibling(h, i).wait_recv()
        both = rb[h, i, :, :, mc] + e1r[h, i]

        @pl.when(i < 3)
        def _():
            v = both.reshape(8, 32, 512)
            most = most_of(v, 1)
            pq[h, i] = coded(v, most).reshape(4, 2, 32, 512)
            ps[h, i] = most.reshape(8, 512)
            for go in along(h, i):
                go.start()

        @pl.when(i == 3)
        def _():
            acc[h] = both

    def second_step(i, carry):
        for h in range(2):

            @pl.when(i < 4)
            def _():
                second(h, i)
                to_sibling(h, i).start()

            @pl.when(i > 0)
            def _():
                add_up(h, i - 1)

        @pl.when(i == 1)
        def _():
            sum_z.wait_recv()
            sx[g] = sz[...] + szr[...]
            for d in ORDER:
                sum_g(d).start()
            for d in ORDER:
                send_h2(d).start()

        @pl.when(i == 3)
        def _():
            for d in ORDER:
                sum_g(d).wait_recv()
            sg[mc, mx] = sx[0] + sx[1] + sx[2] + sx[3]
            for d in ORDER:
                all_x(d).start()

        return carry

    lax.fori_loop(0, 5, second_step, 0)

    def across(h, d):
        to = to_y(d) if h == 0 else to_x(d)
        k = 3 * h + d - 1
        return (
            copy(aq.at[h, d - 1], aqr.at[h, d - 1], "q", k, to),
            copy(aps.at[h, d - 1], apr.at[h, d - 1], "qs", k, to),
        )

    for i in range(3):
        for h in range(2):
            for go in along(h, i):
                go.wait_recv()
            more = decoded(pqr[h, i].reshape(8, 32, 512), psr[h, i].reshape(8, 1, 512))
            acc[h] += more.reshape(4, 2, 32, 512)
            if i == 2:
                for d in ORDER:
                    v = acc[h, at_y(d) if h == 0 else at_x(d)]
                    most = most_of(v, 1)
                    aq[h, d - 1] = coded(v, most)
                    aps[h, d - 1] = jnp.broadcast_to(most, (2, 8, 512))
                    for go in across(h, d):
                        go.start()
    for d in ORDER:
        all_x(d).wait_recv()
    all_c.start()
    for d in ORDER:
        send_h2(d).wait_recv()
    for j in range(NG):
        h2_out[:, 128 * j : 128 * j + 128] = h2b[j]
    rowsum = jnp.concatenate([sg[mc, mx, k : k + 1, 640:768] for k in range(4)], axis=1)
    for h in range(2):
        whole = acc[h, my if h == 0 else mx]
        for d in ORDER:
            for go in across(h, d):
                go.wait_recv()
            whole += decoded(aqr[h, d - 1], apr[h, d - 1, :, 0:1])
        fin[:, h] = whole
    most = most_of(fin[oz], 1)
    lq[...] = coded(fin[oz], most)
    lps[...] = jnp.broadcast_to(most, (2, 8, 512))
    last = (copy(lq, lqr, "l", 0, z_pair), copy(lps, lpr, "ls", 0, z_pair))
    for go in last:
        go.start()
    all_c.wait_recv()
    for j in range(NG):
        for c in range(NC):
            at = slice(16 * j + 8 * c, 16 * j + 8 * c + 8)
            w2t_out[at, :] = w2tv[at, :] * sg[c, j, :, 0:512] / sg[c, j, :, 512:513]
    for go in last:
        go.wait_recv()
    w1_num = (fin[mz] + decoded(lqr[...], lpr[:, 0:1])).reshape(64, 512)
    w1_now = wg[mx, my, mz, mc].astype(F32).reshape(64, 512)
    w1_out[...] = (w1_now * w1_num / rowsum).astype(BF16)

    for sent in (go_z, sum_c, sum_z, all_c) + last:
        sent.wait_send()
    for d in ORDER:
        for h in range(2):
            for sent in (near(0, h, d), near(1, h, d), send_hs(h, d)):
                sent.wait_send()
            for e in ORDER:
                far(0, h, e, d).wait_send()
                far(1, h, e, d).wait_send()
            for sent in along(h, d - 1) + across(h, d):
                sent.wait_send()
        for sent in (send_marks, send_h2, sum_g, sum_x, sum_y, all_x):
            sent(d).wait_send()
    for b in range(2):
        for p in range(2):
            for sent in (send_diag(b, p), pass_h(b, p), send_h(b, 3 if p else 1)):
                sent.wait_send()
            for d in (1, 3):
                send_num(b, d, p).wait_send()
    for h in range(2):
        for d in range(4):
            forward(h, d).wait_send()
            to_sibling(h, d).wait_send()


def finish(w1, h1, w2t, h2, w1_out, h1_out, w2t_out, h2_out, sem):
    pairs = ((h1, h1_out), (w1, w1_out), (w2t, w2t_out), (h2, h2_out))
    stores = [pltpu.make_async_copy(a, b, sem.at[k]) for k, (a, b) in enumerate(pairs)]
    for go in stores:
        go.start()
    for go in stores:
        go.wait()


def on_device(counts, w1, h1, w2, h2):
    anywhere = pl.BlockSpec(memory_space=pl.ANY)
    vmem = pl.BlockSpec(memory_space=pltpu.VMEM)
    shape = (NX, NY, NZ, NC, 2, 32, 512)
    sds = jax.ShapeDtypeStruct
    outs = (
        sds((64, 512), BF16),
        sds((512, 512), F32),
        sds((64, 512), F32),
        sds((64, 512), F32),
    )
    scratch = [
        (shape, BF16), (shape, jnp.int32), ((512, 512), F32), ((64, 512), F32), ((64, 512), F32),
        ((512, 512), BF16), ((NG, 512, 128), F32), ((3, 512, 128), I16), ((3, 512, 128), I16),
        ((3, 8, 768), F32), ((3, 8, 768), F32), ((8, 512), F32),
        ((512, 128), F32), ((2, NG, 256, 128), I16), ((2, NG, 8, 128), F32), ((NG, 64, 128), F32),
        ((2, 4, 4, 2, 2, 32, 512), F32), ((2, 4, 4, 2, 32, 512), F32), ((2, 4, 2, 32, 512), F32),
        ((2, 3, 4, 2, 32, 512), I16), ((2, 3, 4, 2, 32, 512), I16), ((2, 3, 8, 512), F32), ((2, 3, 8, 512), F32),
        ((2, 3, 2, 32, 512), I16), ((2, 3, 2, 32, 512), I16), ((2, 3, 2, 8, 512), F32), ((2, 3, 2, 8, 512), F32),
        ((2, 2, 32, 512), F32), ((2, 32, 512), I16), ((2, 32, 512), I16), ((2, 8, 512), F32), ((2, 8, 512), F32),
        ((2, NG, 8, 768), F32), ((NG, 8, 768), F32), ((NG, 8, 768), F32), ((3, 8, 768), F32), ((8, 768), F32),
        ((8, 768), F32), ((4, 8, 768), F32), ((4, 8, 768), F32), ((2, NG, 8, 768), F32),
    ]
    moved = pl.pallas_call(
        kernel,
        out_shape=tuple(pltpu.VMEM(o.shape, o.dtype) for o in outs),
        in_specs=[anywhere] * 5,
        out_specs=(vmem,) * 4,
        scratch_shapes=[pltpu.VMEM(*s) for s in scratch]
        + [
            pltpu.SemaphoreType.DMA((S_ALL,)),
            pltpu.SemaphoreType.DMA((S_ALL,)),
            pltpu.SemaphoreType.DMA((5,)),
        ],
        compiler_params=pltpu.CompilerParams(
            collective_id=0, has_side_effects=True, vmem_limit_bytes=56 * 1024 * 1024
        ),
    )(counts.reshape(shape), w1.reshape(2, 32, 512), h1, w2.T, h2)
    w1_new, h1_new, w2t_new, h2_new = pl.pallas_call(
        finish,
        out_shape=outs,
        in_specs=[vmem] * 4,
        out_specs=(anywhere,) * 4,
        scratch_shapes=[pltpu.SemaphoreType.DMA((4,))],
    )(*[pltpu.with_memory_space_constraint(m, pltpu.VMEM) for m in moved])
    return w1_new, h1_new, w2t_new.T, h2_new


def solution(mesh):
    placed = (P("gene", "cell"), P(("gene", "cell"), None), P(None, "cell"), P(), P(None, "cell"))
    return jax.shard_map(
        on_device,
        mesh=mesh,
        in_specs=placed,
        out_specs=(P(("gene", "cell"), None), P(None, "cell"), P(), P(None, "cell")),
        check_vma=False,
    )
```

```python
import jax
import jax.numpy as jnp
from jax import lax
from jax.experimental import pallas as pl
from jax.experimental.pallas import tpu as pltpu
from jax.sharding import PartitionSpec as P

NX, NY, NZ, NC = 4, 4, 2, 2
NG = 4
F32, BF16, I16 = jnp.float32, jnp.bfloat16, jnp.int16
HI = lax.Precision.HIGHEST
TOP = 32767.0
ORDER = (1, 3, 2)

SIZES = dict(
    z=1, a2=12, a3=36, f=8, m=3, nd=4, n=8, hb=4, hf=4, hs=6, h2=3, e1=8, pd=4, pds=4, p=8, ps=4, q=6, qs=6, l=1, ls=1,
    s0=1, s1=3, s2=3, s3=1, s4=3, s5=3, s6=1,
)
PLACE, S_ALL = {}, 0
for _name, _size in SIZES.items():
    PLACE[_name] = S_ALL
    S_ALL += _size


def nt(a, b, precision=None):
    return lax.dot_general(
        a, b, (((1,), (1,)), ((), ())), preferred_element_type=F32, precision=precision
    )


def high(a, b):
    return jnp.dot(a, b, precision=HI, preferred_element_type=F32)


def most_of(v, axis):
    return jnp.maximum(jnp.max(v, axis=axis, keepdims=True), 1e-30)


def coded(v, most):
    return jnp.round(v * (TOP / most)).astype(jnp.int32).astype(I16)


def coded_by_8(v):
    rows = v.reshape(8, 8, 512)
    most = most_of(rows, 1)
    whole = jnp.round(rows * (TOP / most)).astype(jnp.int32)
    return whole.reshape(v.shape).astype(I16), most.reshape(8, 512)


def decoded_by_8(q, most):
    whole = q.astype(jnp.int32).astype(F32).reshape(8, 8, 512)
    return (whole * (most.reshape(8, 1, 512) * (1.0 / TOP))).reshape(q.shape)


def decoded(q, most):
    return q.astype(jnp.int32).astype(F32) * (most * (1.0 / TOP))


def kernel(
    counts, w1, h1, w2t, h2,
    w1_out, h1_out, w2t_out, h2_out,
    wg, cnt, h1v, w2tv, h2v, hl, num, nq, nqr, nm, nmr, cs, fr, hq, hs, h2b,
    rb, e1r, acc, pq, pqr, ps, psr, psd, held, aq, aqr, aps, apr, fin, lq, lqr, lps, lpr,
    sm, smr, sv, svr, sz, szr, sx, sy, sg,
    snd, rcv, loc,
):
    g = lax.axis_index("gene")
    ci = lax.axis_index("cell")
    mx, my, mz, mc = ci // 16, (ci // 4) % 4, (ci // 2) % 2, ci % 2
    oz, oc = 1 - mz, 1 - mc

    def cell(x, y, z, c):
        return ((x * NY + y) * NZ + z) * NC + c

    def at_x(d):
        return (mx + d) % NX

    def at_y(d):
        return (my + d) % NY

    def at_g(d):
        return (g + d) % NG

    def copy(src, dst, name, k, to):
        sem = PLACE[name] + k
        return pltpu.make_async_remote_copy(
            src_ref=src,
            dst_ref=dst,
            send_sem=snd.at[sem],
            recv_sem=rcv.at[sem],
            device_id=to,
            device_id_type=pl.DeviceIdType.MESH,
        )

    sibling = (g, cell(mx, my, mz, oc))
    z_pair = (g, cell(mx, my, oz, mc))

    def to_x(d):
        return (g, cell(at_x(d), my, mz, mc))

    def to_y(d):
        return (g, cell(mx, at_y(d), mz, mc))

    def to_g(d):
        return (at_g(d), ci)

    own = wg.at[mx, my, mz, mc]
    barrier = pltpu.get_barrier_semaphore()
    partners = [sibling, z_pair]
    for d in range(1, 4):
        partners += [to_x(d), to_y(d), to_g(d)]
    for to in partners:
        pl.semaphore_signal(barrier, inc=1, device_id=to, device_id_type=pl.DeviceIdType.MESH)
    read_w1 = pltpu.make_async_copy(w1, own, loc.at[0])
    read_h1 = pltpu.make_async_copy(h1, h1v, loc.at[1])
    read_w2 = pltpu.make_async_copy(w2t, w2tv, loc.at[2])
    read_h2 = pltpu.make_async_copy(h2, h2v, loc.at[3])
    read_counts = pltpu.make_async_copy(counts, cnt, loc.at[4])
    for read in (read_w1, read_h1, read_w2, read_h2, read_counts):
        read.start()
    read_w1.wait()
    pl.semaphore_wait(barrier, len(partners))

    go_z = copy(own, own, "z", 0, z_pair)
    go_z.start()

    def near(k, a, d):
        src = wg.at[mx, my, oz if k else mz, mc]
        return copy(src, src, "a2", 6 * k + 3 * a + d - 1, to_y(d) if a else to_x(d))

    for d in ORDER:
        for a in range(2):
            near(0, a, d).start()
    read_h1.wait()
    hl[...] = h1v[...].astype(BF16)
    num[...] = jnp.zeros_like(num)
    cs[...] = jnp.zeros_like(cs)
    go_z.wait_recv()
    for d in ORDER:
        for a in range(2):
            near(1, a, d).start()

    def column(h, d):
        return wg.at[:, at_y(4 - d), :, mc, 0] if h == 0 else wg.at[at_x(4 - d), :, :, mc, 1]

    def far(k, h, e, d):
        z = oz if k else mz
        src = wg.at[mx, at_y(4 - e), z, mc, 1] if h else wg.at[at_x(4 - e), my, z, mc, 0]
        to = to_x(d) if h else to_y(d)
        return copy(src, src, "a3", 18 * k + 9 * h + 3 * (e - 1) + d - 1, to)

    def forward(h, d):
        src = column(h, d)
        return copy(src, src, "f", 4 * h + d, sibling)

    for k in range(2):
        for e in ORDER:
            for h in range(2):
                near(k, h, e).wait_recv()
                for d in (1, 3):
                    far(k, h, e, d).start()
    for k in range(2):
        for e in ORDER:
            for h in range(2):
                far(k, h, e, 2).start()
    for h in range(2):
        forward(h, 0).start()

    read_counts.wait()

    def pass_on(d):
        for h in range(2):
            for e in ORDER:
                far(0, h, e, d).wait_recv()
                far(1, h, e, d).wait_recv()
            forward(h, d).start()

    def first(w, v):
        approx = jnp.dot(w, hl[...], preferred_element_type=F32)
        ratio = (v.astype(F32) / approx).astype(BF16)
        add = lax.dot_general(
            w, ratio, (((0,), (0,)), ((), ())), preferred_element_type=F32
        )
        for j in range(NG):
            num[j] += add[:, j * 128 : (j + 1) * 128]
        cs[...] += jnp.sum(w.astype(F32).reshape(-1, 8, w.shape[1]), axis=0)

    def first_step(t, carry):
        d = t + t // 2 - 2 * (t // 3)
        forward(0, d).wait_recv()
        first(
            wg[:, at_y(4 - d), :, :, 0].reshape(512, 512),
            cnt[:, at_y(4 - d), :, :, 0].reshape(512, 512),
        )
        forward(1, d).wait_recv()
        first(
            wg[at_x(4 - d), :, :, :, 1].reshape(512, 512),
            cnt[at_x(4 - d), :, :, :, 1].reshape(512, 512),
        )

        @pl.when(t == 0)
        def _():
            pass_on(1)
            pass_on(3)

        @pl.when(t == 1)
        def _():
            pass_on(2)

        return carry

    lax.fori_loop(0, 4, first_step, 0)

    def rows(b, p):
        return slice(256 * b + 128 * p, 256 * b + 128 * p + 128)

    def send_marks(d):
        return copy(nm.at[d - 1], nmr.at[d - 1], "m", d - 1, to_g(d))

    def send_diag(b, p):
        at = rows(b, p)
        return copy(nq.at[1, at], nqr.at[1, at], "nd", 2 * b + p, to_g(3 if p else 1))

    def send_num(b, d, p):
        at = rows(b, p)
        return copy(nq.at[d - 1, at], nqr.at[d - 1, at], "n", 4 * b + 2 * p + d // 3, to_g(d))

    def send_h(b, d):
        return copy(hq.at[b, g], hq.at[b, g], "hb", 2 * b + d // 3, to_g(d))

    def send_hs(b, d):
        return copy(hs.at[b, g], hs.at[b, g], "hs", 3 * b + d - 1, to_g(d))

    def pass_h(b, p):
        src = hq.at[b, at_g(1 if p else 3), 128 * p : 128 * p + 128]
        return copy(src, src, "hf", 2 * b + p, to_g(3 if p else 1))

    far_most = most_of(num[at_g(2)], 0)
    for d in (2, 1, 3):
        most = far_most if d == 2 else most_of(num[at_g(d)], 0)
        nm[d - 1, :, 0:512] = cs[...]
        nm[d - 1, :, 512:640] = jnp.broadcast_to(most, (8, 128))
        nm[d - 1, :, 640:768] = jnp.broadcast_to(far_most, (8, 128))
        send_marks(d).start()

    def code_num(b, d, p, more, most):
        at = rows(b, p)
        value = num[at_g(d), at]
        if more is not None:
            value += decoded(nqr[1, at], more)
        nq[d - 1, at] = coded(value, most)

    def mark(d):
        return nm[d - 1, 0:1, 512:640]

    def sent_mark(d, k=0):
        return nmr[d - 1, 0:1, 512 + 128 * k : 640 + 128 * k]

    def start_diag(b):
        for p in range(2):
            code_num(b, 2, p, None, far_most)
            send_diag(b, p).start()

    def start_own(b):
        for d, p in ((1, 1), (3, 0)):
            code_num(b, d, p, None, mark(d))
            send_num(b, d, p).start()

    def start_joined(b):
        for d, p in ((1, 0), (3, 1)):
            send_diag(b, p).wait_recv()
            code_num(b, d, p, sent_mark(d, 1), mark(d) + sent_mark(d, 1))
            send_num(b, d, p).start()

    start_diag(0)
    start_own(0)
    start_diag(1)
    read_w2.wait()
    read_h2.wait()
    w2 = jnp.transpose(w2tv[...])
    mine = pl.ds(pl.multiple_of(g * 128, 128), 128)
    h2_mine = h2v[:, mine]
    fit = high(w2, h2_mine)
    for d in ORDER:
        send_marks(d).wait_recv()
    start_joined(0)
    start_own(1)
    start_joined(1)
    parts = cs[...] + nmr[0, :, 0:512] + nmr[1, :, 0:512] + nmr[2, :, 0:512]
    total = jnp.sum(parts, axis=0, keepdims=True)
    colsum = jnp.transpose(jnp.broadcast_to(total, (128, 512)))
    for b in range(2):
        for p in range(2):
            at = rows(b, p)
            h1_num = num[g, at]
            for d in (3, 1) if p == 0 else (1, 3):
                send_num(b, d, p).wait_recv()
                joined = (d == 1) == (p == 0)
                most = sent_mark(d) + sent_mark(2) if joined else sent_mark(d)
                h1_num += decoded(nqr[d - 1, at], most)
            fr[at] = h1v[at, mine] * h1_num / colsum[at]
        new = fr[256 * b : 256 * b + 256]
        most = most_of(new, 0)
        hq[b, g] = coded(new, most)
        hs[b, g] = jnp.broadcast_to(most, (8, 128))
        for d in (1, 3):
            send_h(b, d).start()
        for d in ORDER:
            send_hs(b, d).start()

    def take_h(b, d):
        j = at_g(4 - d)
        value = decoded(hq[b, j], hs[b, j, 0:1])
        there = pl.ds(pl.multiple_of(j * 128, 128), 128)
        here = pl.ds(256 * b, 256)
        h1_out[here, there] = value
        hl[here, there] = value.astype(BF16)

    def take_near(b):
        for d in (1, 3):
            send_h(b, d).wait_recv()
            pass_h(b, d // 3).start()
        take_h(b, 0)
        for d in (1, 3):
            send_hs(b, d).wait_recv()
            take_h(b, d)

    def take_far(b):
        send_hs(b, 2).wait_recv()
        for p in range(2):
            pass_h(b, p).wait_recv()
        take_h(b, 2)

    fresh = fr[...]

    ratio3 = fresh / fit
    lift = high(w2tv[...], ratio3)
    h2_new = h2_mine * lift / jnp.sum(w2tv[...], axis=1, keepdims=True)
    h2b[g] = h2_new
    ratio4 = fresh / high(w2, h2_new)
    w2_part = nt(h2_new, ratio4, HI)
    h2_part = jnp.broadcast_to(jnp.sum(h2_new, axis=1, keepdims=True), (64, 128))
    h1_rows = nt(jnp.ones((8, 128), F32), fresh, HI)
    for j in range(NG):
        for c in range(NC):
            at = 16 * j + 8 * c
            sm[c, j, :, 0:512] = w2_part[at : at + 8]
            sm[c, j, :, 512:640] = h2_part[at : at + 8]
            sm[c, j, :, 640:768] = jnp.zeros((8, 128), F32)
            for k in range(4):
                sm[c, j, k : k + 1, 640:768] = h1_rows[0:1, k * 128 : (k + 1) * 128]

    sum_c = copy(sm.at[oc], smr, "s0", 0, sibling)

    def sum_x(d):
        return copy(sv.at[at_x(d)], svr.at[d - 1], "s1", d - 1, to_x(d))

    def sum_y(d):
        return copy(sy.at[my], sy.at[my], "s2", d - 1, to_y(d))

    sum_z = copy(sz, szr, "s3", 0, z_pair)

    def sum_g(d):
        return copy(sx.at[g], sx.at[g], "s4", d - 1, to_g(d))

    def all_x(d):
        return copy(sg.at[mc, mx], sg.at[mc, mx], "s5", d - 1, to_x(d))

    all_c = copy(sg.at[mc], sg.at[mc], "s6", 0, sibling)

    def send_h2(d):
        return copy(h2b.at[g], h2b.at[g], "h2", d - 1, to_g(d))

    sum_c.start()
    take_near(0)
    sum_c.wait_recv()
    sv[...] = sm[mc] + smr[...]
    for d in ORDER:
        sum_x(d).start()
    take_near(1)
    for d in ORDER:
        sum_x(d).wait_recv()
    sy[my] = sv[mx] + svr[0] + svr[1] + svr[2]
    for d in ORDER:
        sum_y(d).start()
    take_far(0)
    take_far(1)

    def place(i):
        return (i + 2 + i // 2 + 2 * (i // 3)) % 4

    def second(h, i):
        d = place(i)
        w = wg[:, at_y(d), :, :, 1] if h else wg[at_x(d), :, :, :, 0]
        v = cnt[:, at_y(d), :, :, 1] if h else cnt[at_x(d), :, :, :, 0]
        approx = jnp.dot(w.reshape(512, 512), hl[...], preferred_element_type=F32)
        ratio = (v.reshape(512, 512).astype(F32) / approx).astype(BF16)
        rb[h, i] = nt(ratio, hl[...]).reshape(4, 2, 2, 32, 512)

    def to_sibling(h, i):
        return copy(rb.at[h, i, :, :, oc], e1r.at[h, i], "e1", 4 * h + i, sibling)

    def to(h, d):
        return to_y(d) if h else to_x(d)

    def half(p):
        return slice(2 * p, 2 * p + 2)

    def two_on(h, p):
        d, k = 3 if p else 1, 2 * h + p
        return (
            copy(pq.at[h, 0, half(p)], pqr.at[h, 0, half(p)], "pd", k, to(h, d)),
            copy(ps.at[h, 0], psd.at[h, p], "pds", k, to(h, d)),
        )

    def direct(h, i, p):
        k = 4 * h + 2 * (i - 1) + p
        return copy(pq.at[h, i, half(p)], pqr.at[h, i, half(p)], "p", k, to(h, place(i)))

    def steps(h, i):
        return copy(ps.at[h, i], psr.at[h, i], "ps", 2 * h + i - 1, to(h, place(i)))

    def code_half(h, i, p, v):
        most = most_of(v, 1)
        pq[h, i, half(p)] = coded(v, most).reshape(2, 2, 32, 512)
        ps[h, i, 4 * p : 4 * p + 4] = most.reshape(4, 512)
        direct(h, i, p).start()

    def add_up(h, i):
        to_sibling(h, i).wait_recv()
        both = rb[h, i, :, :, mc] + e1r[h, i]

        @pl.when(i == 0)
        def _():
            v = both.reshape(8, 32, 512)
            most = most_of(v, 1)
            pq[h, 0] = coded(v, most).reshape(4, 2, 32, 512)
            ps[h, 0] = most.reshape(8, 512)
            for p in range(2):
                for go in two_on(h, p):
                    go.start()

        for k in (1, 2):

            @pl.when(i == k)
            def _():
                code_half(h, k, k - 1, both[half(k - 1)].reshape(4, 32, 512))
                held[h, k - 1] = both[half(2 - k)]

        @pl.when(i == 3)
        def _():
            acc[h] = both

    def join(h, i):
        p = 2 - i
        for go in two_on(h, p):
            go.wait_recv()
        q = pqr[h, 0, half(p)].reshape(4, 32, 512)
        more = decoded(q, psd[h, p, 4 * p : 4 * p + 4].reshape(4, 1, 512))
        code_half(h, i, p, held[h, i - 1].reshape(4, 32, 512) + more)
        steps(h, i).start()

    def second_step(i, carry):
        for h in range(2):

            @pl.when(i < 4)
            def _():
                second(h, i)
                to_sibling(h, i).start()

            @pl.when(i > 0)
            def _():
                add_up(h, i - 1)

        @pl.when(i == 1)
        def _():
            for d in ORDER:
                sum_y(d).wait_recv()
            sz[...] = sy[0] + sy[1] + sy[2] + sy[3]
            sum_z.start()
            for d in ORDER:
                send_h2(d).start()

        @pl.when(i == 3)
        def _():
            sum_z.wait_recv()
            sx[g] = sz[...] + szr[...]
            for d in ORDER:
                sum_g(d).start()

        return carry

    lax.fori_loop(0, 5, second_step, 0)

    def across(h, d):
        to = to_y(d) if h == 0 else to_x(d)
        k = 3 * h + d - 1
        return (
            copy(aq.at[h, d - 1], aqr.at[h, d - 1], "q", k, to),
            copy(aps.at[h, d - 1], apr.at[h, d - 1], "qs", k, to),
        )

    for h in range(2):
        for i in (1, 2):
            join(h, i)
    for d in ORDER:
        sum_g(d).wait_recv()
    sg[mc, mx] = sx[0] + sx[1] + sx[2] + sx[3]
    for d in ORDER:
        all_x(d).start()
    for h in range(2):
        for i in (1, 2):
            for p in range(2):
                direct(h, i, p).wait_recv()
            steps(h, i).wait_recv()
            more = decoded(pqr[h, i].reshape(8, 32, 512), psr[h, i].reshape(8, 1, 512))
            acc[h] += more.reshape(4, 2, 32, 512)
            if i == 2:
                for d in ORDER:
                    v = acc[h, at_y(d) if h == 0 else at_x(d)]
                    aq[h, d - 1], aps[h, d - 1] = coded_by_8(v)
                    for go in across(h, d):
                        go.start()
    for d in ORDER:
        all_x(d).wait_recv()
    all_c.start()
    for d in ORDER:
        send_h2(d).wait_recv()
    for j in range(NG):
        h2_out[:, 128 * j : 128 * j + 128] = h2b[j]
    rowsum = jnp.concatenate([sg[mc, mx, k : k + 1, 640:768] for k in range(4)], axis=1)
    for h in range(2):
        whole = acc[h, my if h == 0 else mx]
        for d in ORDER:
            for go in across(h, d):
                go.wait_recv()
            whole += decoded_by_8(aqr[h, d - 1], apr[h, d - 1])
        fin[:, h] = whole
    lq[...], lps[...] = coded_by_8(fin[oz])
    last = (copy(lq, lqr, "l", 0, z_pair), copy(lps, lpr, "ls", 0, z_pair))
    for go in last:
        go.start()
    all_c.wait_recv()
    for j in range(NG):
        for c in range(NC):
            at = slice(16 * j + 8 * c, 16 * j + 8 * c + 8)
            w2t_out[at, :] = w2tv[at, :] * sg[c, j, :, 0:512] / sg[c, j, :, 512:513]
    for go in last:
        go.wait_recv()
    w1_num = (fin[mz] + decoded_by_8(lqr[...], lpr[...])).reshape(64, 512)
    w1_now = wg[mx, my, mz, mc].astype(F32).reshape(64, 512)
    w1_out[...] = (w1_now * w1_num / rowsum).astype(BF16)

    for sent in (go_z, sum_c, sum_z, all_c) + last:
        sent.wait_send()
    for d in ORDER:
        for h in range(2):
            for sent in (near(0, h, d), near(1, h, d), send_hs(h, d)):
                sent.wait_send()
            for e in ORDER:
                far(0, h, e, d).wait_send()
                far(1, h, e, d).wait_send()
            for sent in across(h, d):
                sent.wait_send()
        for sent in (send_marks, send_h2, sum_g, sum_x, sum_y, all_x):
            sent(d).wait_send()
    for b in range(2):
        for p in range(2):
            for sent in (send_diag(b, p), pass_h(b, p), send_h(b, 3 if p else 1)):
                sent.wait_send()
            for d in (1, 3):
                send_num(b, d, p).wait_send()
    for h in range(2):
        for p in range(2):
            for sent in two_on(h, p) + (direct(h, 1, p), direct(h, 2, p), steps(h, 1 + p)):
                sent.wait_send()
        for d in range(4):
            forward(h, d).wait_send()
            to_sibling(h, d).wait_send()


def finish(w1, h1, w2t, h2, w1_out, h1_out, w2t_out, h2_out, sem):
    pairs = ((h1, h1_out), (w1, w1_out), (w2t, w2t_out), (h2, h2_out))
    stores = [pltpu.make_async_copy(a, b, sem.at[k]) for k, (a, b) in enumerate(pairs)]
    for go in stores:
        go.start()
    for go in stores:
        go.wait()


def on_device(counts, w1, h1, w2, h2):
    anywhere = pl.BlockSpec(memory_space=pl.ANY)
    vmem = pl.BlockSpec(memory_space=pltpu.VMEM)
    shape = (NX, NY, NZ, NC, 2, 32, 512)
    sds = jax.ShapeDtypeStruct
    outs = (
        sds((64, 512), BF16),
        sds((512, 512), F32),
        sds((64, 512), F32),
        sds((64, 512), F32),
    )
    scratch = [
        (shape, BF16), (shape, jnp.int32), ((512, 512), F32), ((64, 512), F32), ((64, 512), F32),
        ((512, 512), BF16), ((NG, 512, 128), F32), ((3, 512, 128), I16), ((3, 512, 128), I16),
        ((3, 8, 768), F32), ((3, 8, 768), F32), ((8, 512), F32),
        ((512, 128), F32), ((2, NG, 256, 128), I16), ((2, NG, 8, 128), F32), ((NG, 64, 128), F32),
        ((2, 4, 4, 2, 2, 32, 512), F32), ((2, 4, 4, 2, 32, 512), F32), ((2, 4, 2, 32, 512), F32),
        ((2, 3, 4, 2, 32, 512), I16), ((2, 3, 4, 2, 32, 512), I16), ((2, 3, 8, 512), F32), ((2, 3, 8, 512), F32),
        ((2, 2, 8, 512), F32), ((2, 2, 2, 2, 32, 512), F32),
        ((2, 3, 2, 32, 512), I16), ((2, 3, 2, 32, 512), I16), ((2, 3, 8, 512), F32), ((2, 3, 8, 512), F32),
        ((2, 2, 32, 512), F32), ((2, 32, 512), I16), ((2, 32, 512), I16), ((8, 512), F32), ((8, 512), F32),
        ((2, NG, 8, 768), F32), ((NG, 8, 768), F32), ((NG, 8, 768), F32), ((3, 8, 768), F32), ((8, 768), F32),
        ((8, 768), F32), ((4, 8, 768), F32), ((4, 8, 768), F32), ((2, NG, 8, 768), F32),
    ]
    moved = pl.pallas_call(
        kernel,
        out_shape=tuple(pltpu.VMEM(o.shape, o.dtype) for o in outs),
        in_specs=[anywhere] * 5,
        out_specs=(vmem,) * 4,
        scratch_shapes=[pltpu.VMEM(*s) for s in scratch]
        + [
            pltpu.SemaphoreType.DMA((S_ALL,)),
            pltpu.SemaphoreType.DMA((S_ALL,)),
            pltpu.SemaphoreType.DMA((5,)),
        ],
        compiler_params=pltpu.CompilerParams(
            collective_id=0, has_side_effects=True, vmem_limit_bytes=56 * 1024 * 1024
        ),
    )(counts.reshape(shape), w1.reshape(2, 32, 512), h1, w2.T, h2)
    w1_new, h1_new, w2t_new, h2_new = pl.pallas_call(
        finish,
        out_shape=outs,
        in_specs=[vmem] * 4,
        out_specs=(anywhere,) * 4,
        scratch_shapes=[pltpu.SemaphoreType.DMA((4,))],
    )(*[pltpu.with_memory_space_constraint(m, pltpu.VMEM) for m in moved])
    return w1_new, h1_new, w2t_new.T, h2_new


def solution(mesh):
    placed = (P("gene", "cell"), P(("gene", "cell"), None), P(None, "cell"), P(), P(None, "cell"))
    return jax.shard_map(
        on_device,
        mesh=mesh,
        in_specs=placed,
        out_specs=(P(("gene", "cell"), None), P(None, "cell"), P(), P(None, "cell")),
        check_vma=False,
    )
```

```python
import jax
import jax.numpy as jnp
from jax import lax
from jax.experimental import pallas as pl
from jax.experimental.pallas import tpu as pltpu
from jax.sharding import PartitionSpec as P

NX, NY, NZ, NC = 4, 4, 2, 2
NG = 4
F32, BF16, I16 = jnp.float32, jnp.bfloat16, jnp.int16
HI = lax.Precision.HIGHEST
TOP = 32767.0
ORDER = (1, 3, 2)

SIZES = dict(
    z=1, a2=12, a3=36, f=8, m=3, nd=4, n=8, hb=4, hf=4, hs=6, h2=3, e1=8, pd=4, pds=4, p=8, ps=4, q=12, qs=6, l=1, ls=1,
    s0=1, s1=3, s2=3, s3=1, s4=3, s5=3, s6=1,
)
PLACE, S_ALL = {}, 0
for _name, _size in SIZES.items():
    PLACE[_name] = S_ALL
    S_ALL += _size


def nt(a, b, precision=None):
    return lax.dot_general(
        a, b, (((1,), (1,)), ((), ())), preferred_element_type=F32, precision=precision
    )


def high(a, b):
    return jnp.dot(a, b, precision=HI, preferred_element_type=F32)


def most_of(v, axis):
    return jnp.maximum(jnp.max(v, axis=axis, keepdims=True), 1e-30)


def coded(v, most):
    return jnp.round(v * (TOP / most)).astype(jnp.int32).astype(I16)


def coded_by_8(v):
    rows = v.reshape(8, 8, 512)
    most = most_of(rows, 1)
    whole = jnp.round(rows * (TOP / most)).astype(jnp.int32)
    return whole.reshape(v.shape).astype(I16), most.reshape(8, 512)


def decoded_by_8(q, most):
    whole = q.astype(jnp.int32).astype(F32).reshape(8, 8, 512)
    return (whole * (most.reshape(8, 1, 512) * (1.0 / TOP))).reshape(q.shape)


def decoded(q, most):
    return q.astype(jnp.int32).astype(F32) * (most * (1.0 / TOP))


def kernel(
    counts, w1, h1, w2t, h2,
    w1_out, h1_out, w2t_out, h2_out,
    wg, cnt, h1v, w2tv, h2v, hl, num, nq, nqr, nm, nmr, cs, fr, hq, hs, h2b,
    rb, e1r, acc, pq, pqr, ps, psr, psd, held, aq, aqr, aps, apr, fin, lq, lqr, lps, lpr,
    sm, smr, sv, svr, sz, szr, sx, sy, sg,
    snd, rcv, loc,
):
    g = lax.axis_index("gene")
    ci = lax.axis_index("cell")
    mx, my, mz, mc = ci // 16, (ci // 4) % 4, (ci // 2) % 2, ci % 2
    oz, oc = 1 - mz, 1 - mc

    def cell(x, y, z, c):
        return ((x * NY + y) * NZ + z) * NC + c

    def at_x(d):
        return (mx + d) % NX

    def at_y(d):
        return (my + d) % NY

    def at_g(d):
        return (g + d) % NG

    def copy(src, dst, name, k, to):
        sem = PLACE[name] + k
        return pltpu.make_async_remote_copy(
            src_ref=src,
            dst_ref=dst,
            send_sem=snd.at[sem],
            recv_sem=rcv.at[sem],
            device_id=to,
            device_id_type=pl.DeviceIdType.MESH,
        )

    sibling = (g, cell(mx, my, mz, oc))
    z_pair = (g, cell(mx, my, oz, mc))

    def to_x(d):
        return (g, cell(at_x(d), my, mz, mc))

    def to_y(d):
        return (g, cell(mx, at_y(d), mz, mc))

    def to_g(d):
        return (at_g(d), ci)

    own = wg.at[mx, my, mz, mc]
    barrier = pltpu.get_barrier_semaphore()
    partners = [sibling, z_pair]
    for d in range(1, 4):
        partners += [to_x(d), to_y(d), to_g(d)]
    for to in partners:
        pl.semaphore_signal(barrier, inc=1, device_id=to, device_id_type=pl.DeviceIdType.MESH)
    read_w1 = pltpu.make_async_copy(w1, own, loc.at[0])
    read_h1 = pltpu.make_async_copy(h1, h1v, loc.at[1])
    read_w2 = pltpu.make_async_copy(w2t, w2tv, loc.at[2])
    read_h2 = pltpu.make_async_copy(h2, h2v, loc.at[3])
    read_counts = pltpu.make_async_copy(counts, cnt, loc.at[4])
    for read in (read_w1, read_h1, read_w2, read_h2, read_counts):
        read.start()
    read_w1.wait()
    pl.semaphore_wait(barrier, len(partners))

    go_z = copy(own, own, "z", 0, z_pair)
    go_z.start()

    def near(k, a, d):
        src = wg.at[mx, my, oz if k else mz, mc]
        return copy(src, src, "a2", 6 * k + 3 * a + d - 1, to_y(d) if a else to_x(d))

    for d in ORDER:
        for a in range(2):
            near(0, a, d).start()
    read_h1.wait()
    hl[...] = h1v[...].astype(BF16)
    num[...] = jnp.zeros_like(num)
    cs[...] = jnp.zeros_like(cs)
    go_z.wait_recv()
    for d in ORDER:
        for a in range(2):
            near(1, a, d).start()

    def column(h, d):
        return wg.at[:, at_y(4 - d), :, mc, 0] if h == 0 else wg.at[at_x(4 - d), :, :, mc, 1]

    def far(k, h, e, d):
        z = oz if k else mz
        src = wg.at[mx, at_y(4 - e), z, mc, 1] if h else wg.at[at_x(4 - e), my, z, mc, 0]
        to = to_x(d) if h else to_y(d)
        return copy(src, src, "a3", 18 * k + 9 * h + 3 * (e - 1) + d - 1, to)

    def forward(h, d):
        src = column(h, d)
        return copy(src, src, "f", 4 * h + d, sibling)

    for k in range(2):
        for e in ORDER:
            for h in range(2):
                near(k, h, e).wait_recv()
                for d in (1, 3):
                    far(k, h, e, d).start()
    for k in range(2):
        for e in ORDER:
            for h in range(2):
                far(k, h, e, 2).start()
    for h in range(2):
        forward(h, 0).start()

    read_counts.wait()

    def pass_on(d):
        for h in range(2):
            for e in ORDER:
                far(0, h, e, d).wait_recv()
                far(1, h, e, d).wait_recv()
            forward(h, d).start()

    def first(w, v):
        approx = jnp.dot(w, hl[...], preferred_element_type=F32)
        ratio = (v.astype(F32) / approx).astype(BF16)
        add = lax.dot_general(
            w, ratio, (((0,), (0,)), ((), ())), preferred_element_type=F32
        )
        for j in range(NG):
            num[j] += add[:, j * 128 : (j + 1) * 128]
        cs[...] += jnp.sum(w.astype(F32).reshape(-1, 8, w.shape[1]), axis=0)

    def first_step(t, carry):
        d = t + t // 2 - 2 * (t // 3)
        forward(0, d).wait_recv()
        first(
            wg[:, at_y(4 - d), :, :, 0].reshape(512, 512),
            cnt[:, at_y(4 - d), :, :, 0].reshape(512, 512),
        )
        forward(1, d).wait_recv()
        first(
            wg[at_x(4 - d), :, :, :, 1].reshape(512, 512),
            cnt[at_x(4 - d), :, :, :, 1].reshape(512, 512),
        )

        @pl.when(t == 0)
        def _():
            pass_on(1)
            pass_on(3)

        @pl.when(t == 1)
        def _():
            pass_on(2)

        return carry

    lax.fori_loop(0, 4, first_step, 0)

    def rows(b, p):
        return slice(256 * b + 128 * p, 256 * b + 128 * p + 128)

    def send_marks(d):
        return copy(nm.at[d - 1], nmr.at[d - 1], "m", d - 1, to_g(d))

    def send_diag(b, p):
        at = rows(b, p)
        return copy(nq.at[1, at], nqr.at[1, at], "nd", 2 * b + p, to_g(3 if p else 1))

    def send_num(b, d, p):
        at = rows(b, p)
        return copy(nq.at[d - 1, at], nqr.at[d - 1, at], "n", 4 * b + 2 * p + d // 3, to_g(d))

    def send_h(b, d):
        return copy(hq.at[b, g], hq.at[b, g], "hb", 2 * b + d // 3, to_g(d))

    def send_hs(b, d):
        return copy(hs.at[b, g], hs.at[b, g], "hs", 3 * b + d - 1, to_g(d))

    def pass_h(b, p):
        src = hq.at[b, at_g(1 if p else 3), 128 * p : 128 * p + 128]
        return copy(src, src, "hf", 2 * b + p, to_g(3 if p else 1))

    far_most = most_of(num[at_g(2)], 0)
    def code_num(b, d, p, more, most):
        at = rows(b, p)
        value = num[at_g(d), at]
        if more is not None:
            value += decoded(nqr[1, at], more)
        nq[d - 1, at] = coded(value, most)

    def start_diag(b):
        for p in range(2):
            code_num(b, 2, p, None, far_most)
            send_diag(b, p).start()

    start_diag(0)
    for d in (2, 1, 3):
        most = far_most if d == 2 else most_of(num[at_g(d)], 0)
        nm[d - 1, :, 0:512] = cs[...]
        nm[d - 1, :, 512:640] = jnp.broadcast_to(most, (8, 128))
        nm[d - 1, :, 640:768] = jnp.broadcast_to(far_most, (8, 128))
        send_marks(d).start()

    def mark(d):
        return nm[d - 1, 0:1, 512:640]

    def sent_mark(d, k=0):
        return nmr[d - 1, 0:1, 512 + 128 * k : 640 + 128 * k]

    def start_own(b):
        for d, p in ((1, 1), (3, 0)):
            code_num(b, d, p, None, mark(d))
            send_num(b, d, p).start()

    def start_joined(b):
        for d, p in ((1, 0), (3, 1)):
            send_diag(b, p).wait_recv()
            code_num(b, d, p, sent_mark(d, 1), mark(d) + sent_mark(d, 1))
            send_num(b, d, p).start()

    start_own(0)
    start_diag(1)
    read_w2.wait()
    read_h2.wait()
    w2 = jnp.transpose(w2tv[...])
    mine = pl.ds(pl.multiple_of(g * 128, 128), 128)
    h2_mine = h2v[:, mine]
    fit = high(w2, h2_mine)
    for d in ORDER:
        send_marks(d).wait_recv()
    start_joined(0)
    start_own(1)
    start_joined(1)
    parts = cs[...] + nmr[0, :, 0:512] + nmr[1, :, 0:512] + nmr[2, :, 0:512]
    total = jnp.sum(parts, axis=0, keepdims=True)
    colsum = jnp.transpose(jnp.broadcast_to(total, (128, 512)))
    for b in range(2):
        for p in range(2):
            at = rows(b, p)
            h1_num = num[g, at]
            for d in (3, 1) if p == 0 else (1, 3):
                send_num(b, d, p).wait_recv()
                joined = (d == 1) == (p == 0)
                most = sent_mark(d) + sent_mark(2) if joined else sent_mark(d)
                h1_num += decoded(nqr[d - 1, at], most)
            fr[at] = h1v[at, mine] * h1_num / colsum[at]
        new = fr[256 * b : 256 * b + 256]
        most = most_of(new, 0)
        hq[b, g] = coded(new, most)
        hs[b, g] = jnp.broadcast_to(most, (8, 128))
        for d in (1, 3):
            send_h(b, d).start()
        for d in ORDER:
            send_hs(b, d).start()

    def take_h(b, d):
        j = at_g(4 - d)
        value = decoded(hq[b, j], hs[b, j, 0:1])
        there = pl.ds(pl.multiple_of(j * 128, 128), 128)
        here = pl.ds(256 * b, 256)
        h1_out[here, there] = value
        hl[here, there] = value.astype(BF16)

    def take_near(b):
        for d in (1, 3):
            send_h(b, d).wait_recv()
            pass_h(b, d // 3).start()
        take_h(b, 0)
        for d in (1, 3):
            send_hs(b, d).wait_recv()
            take_h(b, d)

    def take_far(b):
        send_hs(b, 2).wait_recv()
        for p in range(2):
            pass_h(b, p).wait_recv()
        take_h(b, 2)

    fresh = fr[...]

    ratio3 = fresh / fit
    lift = high(w2tv[...], ratio3)
    h2_new = h2_mine * lift / jnp.sum(w2tv[...], axis=1, keepdims=True)
    h2b[g] = h2_new
    ratio4 = fresh / high(w2, h2_new)
    w2_part = nt(h2_new, ratio4, HI)
    h2_part = jnp.broadcast_to(jnp.sum(h2_new, axis=1, keepdims=True), (64, 128))
    h1_rows = nt(jnp.ones((8, 128), F32), fresh, HI)
    for j in range(NG):
        for c in range(NC):
            at = 16 * j + 8 * c
            sm[c, j, :, 0:512] = w2_part[at : at + 8]
            sm[c, j, :, 512:640] = h2_part[at : at + 8]
            sm[c, j, :, 640:768] = jnp.zeros((8, 128), F32)
            for k in range(4):
                sm[c, j, k : k + 1, 640:768] = h1_rows[0:1, k * 128 : (k + 1) * 128]

    sum_c = copy(sm.at[oc], smr, "s0", 0, sibling)

    def sum_x(d):
        return copy(sv.at[at_x(d)], svr.at[d - 1], "s1", d - 1, to_x(d))

    def sum_y(d):
        return copy(sy.at[my], sy.at[my], "s2", d - 1, to_y(d))

    sum_z = copy(sz, szr, "s3", 0, z_pair)

    def sum_g(d):
        return copy(sx.at[g], sx.at[g], "s4", d - 1, to_g(d))

    def all_x(d):
        return copy(sg.at[mc, mx], sg.at[mc, mx], "s5", d - 1, to_x(d))

    all_c = copy(sg.at[mc], sg.at[mc], "s6", 0, sibling)

    def send_h2(d):
        return copy(h2b.at[g], h2b.at[g], "h2", d - 1, to_g(d))

    sum_c.start()
    take_near(0)
    sum_c.wait_recv()
    sv[...] = sm[mc] + smr[...]
    for d in ORDER:
        sum_x(d).start()
    take_near(1)
    for d in ORDER:
        sum_x(d).wait_recv()
    sy[my] = sv[mx] + svr[0] + svr[1] + svr[2]
    for d in ORDER:
        sum_y(d).start()
    take_far(0)
    take_far(1)

    def place(i):
        return (i + 2 + i // 2 + 2 * (i // 3)) % 4

    def second(h, i):
        d = place(i)
        w = wg[:, at_y(d), :, :, 1] if h else wg[at_x(d), :, :, :, 0]
        v = cnt[:, at_y(d), :, :, 1] if h else cnt[at_x(d), :, :, :, 0]
        approx = jnp.dot(w.reshape(512, 512), hl[...], preferred_element_type=F32)
        ratio = (v.reshape(512, 512).astype(F32) / approx).astype(BF16)
        rb[h, i] = nt(ratio, hl[...]).reshape(4, 2, 2, 32, 512)

    def to_sibling(h, i):
        return copy(rb.at[h, i, :, :, oc], e1r.at[h, i], "e1", 4 * h + i, sibling)

    def to(h, d):
        return to_y(d) if h else to_x(d)

    def half(p):
        return slice(2 * p, 2 * p + 2)

    def two_on(h, p):
        d, k = 3 if p else 1, 2 * h + p
        return (
            copy(pq.at[h, 0, half(p)], pqr.at[h, 0, half(p)], "pd", k, to(h, d)),
            copy(ps.at[h, 0], psd.at[h, p], "pds", k, to(h, d)),
        )

    def direct(h, i, p):
        k = 4 * h + 2 * (i - 1) + p
        return copy(pq.at[h, i, half(p)], pqr.at[h, i, half(p)], "p", k, to(h, place(i)))

    def steps(h, i):
        return copy(ps.at[h, i], psr.at[h, i], "ps", 2 * h + i - 1, to(h, place(i)))

    def code_half(h, i, p, v):
        most = most_of(v, 1)
        pq[h, i, half(p)] = coded(v, most).reshape(2, 2, 32, 512)
        ps[h, i, 4 * p : 4 * p + 4] = most.reshape(4, 512)
        direct(h, i, p).start()

    def add_up(h, i):
        to_sibling(h, i).wait_recv()
        both = rb[h, i, :, :, mc] + e1r[h, i]

        @pl.when(i == 0)
        def _():
            v = both.reshape(8, 32, 512)
            most = most_of(v, 1)
            pq[h, 0] = coded(v, most).reshape(4, 2, 32, 512)
            ps[h, 0] = most.reshape(8, 512)
            for p in range(2):
                for go in two_on(h, p):
                    go.start()

        for k in (1, 2):

            @pl.when(i == k)
            def _():
                code_half(h, k, k - 1, both[half(k - 1)].reshape(4, 32, 512))
                held[h, k - 1] = both[half(2 - k)]

        @pl.when(i == 3)
        def _():
            acc[h] = both

    def join(h, i):
        p = 2 - i
        for go in two_on(h, p):
            go.wait_recv()
        q = pqr[h, 0, half(p)].reshape(4, 32, 512)
        more = decoded(q, psd[h, p, 4 * p : 4 * p + 4].reshape(4, 1, 512))
        code_half(h, i, p, held[h, i - 1].reshape(4, 32, 512) + more)
        steps(h, i).start()

    def second_step(i, carry):
        for h in range(2):

            @pl.when(i < 4)
            def _():
                second(h, i)
                to_sibling(h, i).start()

            @pl.when(i > 0)
            def _():
                add_up(h, i - 1)

        @pl.when(i == 1)
        def _():
            for d in ORDER:
                sum_y(d).wait_recv()
            sz[...] = sy[0] + sy[1] + sy[2] + sy[3]
            sum_z.start()
            for d in ORDER:
                send_h2(d).start()

        @pl.when(i == 3)
        def _():
            sum_z.wait_recv()
            sx[g] = sz[...] + szr[...]
            for d in ORDER:
                sum_g(d).start()

        return carry

    lax.fori_loop(0, 5, second_step, 0)

    def across(h, d, s):
        k = 6 * h + 2 * (d - 1) + s
        return copy(aq.at[h, d - 1, s], aqr.at[h, d - 1, s], "q", k, to(1 - h, d))

    def across_steps(h, d):
        k = 3 * h + d - 1
        return copy(aps.at[h, d - 1], apr.at[h, d - 1], "qs", k, to(1 - h, d))

    def add_across(h, s):
        whole = acc[h, my if h == 0 else mx, mz if s else oz].reshape(4, 8, 512)
        for d in ORDER:
            across(h, d, s).wait_recv()
            if s == 0:
                across_steps(h, d).wait_recv()
            q = aqr[h, d - 1, s].astype(jnp.int32).astype(F32).reshape(4, 8, 512)
            most = apr[h, d - 1, 4 * s : 4 * s + 4].reshape(4, 1, 512)
            whole += q * (most * (1.0 / TOP))
        fin[s, h] = whole.reshape(32, 512)

    for h in range(2):
        for i in (1, 2):
            join(h, i)
    for d in ORDER:
        sum_g(d).wait_recv()
    sg[mc, mx] = sx[0] + sx[1] + sx[2] + sx[3]
    for d in ORDER:
        all_x(d).start()
    for h in range(2):
        for i in (1, 2):
            for p in range(2):
                direct(h, i, p).wait_recv()
            steps(h, i).wait_recv()
            more = decoded(pqr[h, i].reshape(8, 32, 512), psr[h, i].reshape(8, 1, 512))
            acc[h] += more.reshape(4, 2, 32, 512)
            if i == 2:
                for s in range(2):
                    for d in ORDER:
                        v = acc[h, at_y(d) if h == 0 else at_x(d), mz if s else oz].reshape(4, 8, 512)
                        most = most_of(v, 1)
                        whole = jnp.round(v * (TOP / most)).astype(jnp.int32)
                        aq[h, d - 1, s] = whole.reshape(32, 512).astype(I16)
                        aps[h, d - 1, 4 * s : 4 * s + 4] = most.reshape(4, 512)
                        if s == 0:
                            across(h, d, 0).start()
                for d in ORDER:
                    across_steps(h, d).start()
                for d in ORDER:
                    across(h, d, 1).start()
    for d in ORDER:
        all_x(d).wait_recv()
    all_c.start()
    for d in ORDER:
        send_h2(d).wait_recv()
    for j in range(NG):
        h2_out[:, 128 * j : 128 * j + 128] = h2b[j]
    rowsum = jnp.concatenate([sg[mc, mx, k : k + 1, 640:768] for k in range(4)], axis=1)
    for h in range(2):
        add_across(h, 0)
    lq[...], lps[...] = coded_by_8(fin[0])
    last = (copy(lq, lqr, "l", 0, z_pair), copy(lps, lpr, "ls", 0, z_pair))
    for go in last:
        go.start()
    for h in range(2):
        add_across(h, 1)
    all_c.wait_recv()
    for j in range(NG):
        for c in range(NC):
            at = slice(16 * j + 8 * c, 16 * j + 8 * c + 8)
            w2t_out[at, :] = w2tv[at, :] * sg[c, j, :, 0:512] / sg[c, j, :, 512:513]
    for go in last:
        go.wait_recv()
    w1_num = (fin[1] + decoded_by_8(lqr[...], lpr[...])).reshape(64, 512)
    w1_now = wg[mx, my, mz, mc].astype(F32).reshape(64, 512)
    w1_out[...] = (w1_now * w1_num / rowsum).astype(BF16)

    for sent in (go_z, sum_c, sum_z, all_c) + last:
        sent.wait_send()
    for d in ORDER:
        for h in range(2):
            for sent in (near(0, h, d), near(1, h, d), send_hs(h, d)):
                sent.wait_send()
            for e in ORDER:
                far(0, h, e, d).wait_send()
                far(1, h, e, d).wait_send()
            for sent in (across(h, d, 0), across(h, d, 1), across_steps(h, d)):
                sent.wait_send()
        for sent in (send_marks, send_h2, sum_g, sum_x, sum_y, all_x):
            sent(d).wait_send()
    for b in range(2):
        for p in range(2):
            for sent in (send_diag(b, p), pass_h(b, p), send_h(b, 3 if p else 1)):
                sent.wait_send()
            for d in (1, 3):
                send_num(b, d, p).wait_send()
    for h in range(2):
        for p in range(2):
            for sent in two_on(h, p) + (direct(h, 1, p), direct(h, 2, p), steps(h, 1 + p)):
                sent.wait_send()
        for d in range(4):
            forward(h, d).wait_send()
            to_sibling(h, d).wait_send()


def finish(w1, h1, w2t, h2, w1_out, h1_out, w2t_out, h2_out, sem):
    pairs = ((h1, h1_out), (w1, w1_out), (w2t, w2t_out), (h2, h2_out))
    stores = [pltpu.make_async_copy(a, b, sem.at[k]) for k, (a, b) in enumerate(pairs)]
    for go in stores:
        go.start()
    for go in stores:
        go.wait()


def on_device(counts, w1, h1, w2, h2):
    anywhere = pl.BlockSpec(memory_space=pl.ANY)
    vmem = pl.BlockSpec(memory_space=pltpu.VMEM)
    shape = (NX, NY, NZ, NC, 2, 32, 512)
    sds = jax.ShapeDtypeStruct
    outs = (
        sds((64, 512), BF16),
        sds((512, 512), F32),
        sds((64, 512), F32),
        sds((64, 512), F32),
    )
    scratch = [
        (shape, BF16), (shape, jnp.int32), ((512, 512), F32), ((64, 512), F32), ((64, 512), F32),
        ((512, 512), BF16), ((NG, 512, 128), F32), ((3, 512, 128), I16), ((3, 512, 128), I16),
        ((3, 8, 768), F32), ((3, 8, 768), F32), ((8, 512), F32),
        ((512, 128), F32), ((2, NG, 256, 128), I16), ((2, NG, 8, 128), F32), ((NG, 64, 128), F32),
        ((2, 4, 4, 2, 2, 32, 512), F32), ((2, 4, 4, 2, 32, 512), F32), ((2, 4, 2, 32, 512), F32),
        ((2, 3, 4, 2, 32, 512), I16), ((2, 3, 4, 2, 32, 512), I16), ((2, 3, 8, 512), F32), ((2, 3, 8, 512), F32),
        ((2, 2, 8, 512), F32), ((2, 2, 2, 2, 32, 512), F32),
        ((2, 3, 2, 32, 512), I16), ((2, 3, 2, 32, 512), I16), ((2, 3, 8, 512), F32), ((2, 3, 8, 512), F32),
        ((2, 2, 32, 512), F32), ((2, 32, 512), I16), ((2, 32, 512), I16), ((8, 512), F32), ((8, 512), F32),
        ((2, NG, 8, 768), F32), ((NG, 8, 768), F32), ((NG, 8, 768), F32), ((3, 8, 768), F32), ((8, 768), F32),
        ((8, 768), F32), ((4, 8, 768), F32), ((4, 8, 768), F32), ((2, NG, 8, 768), F32),
    ]
    moved = pl.pallas_call(
        kernel,
        out_shape=tuple(pltpu.VMEM(o.shape, o.dtype) for o in outs),
        in_specs=[anywhere] * 5,
        out_specs=(vmem,) * 4,
        scratch_shapes=[pltpu.VMEM(*s) for s in scratch]
        + [
            pltpu.SemaphoreType.DMA((S_ALL,)),
            pltpu.SemaphoreType.DMA((S_ALL,)),
            pltpu.SemaphoreType.DMA((5,)),
        ],
        compiler_params=pltpu.CompilerParams(
            collective_id=0, has_side_effects=True, vmem_limit_bytes=56 * 1024 * 1024
        ),
    )(counts.reshape(shape), w1.reshape(2, 32, 512), h1, w2.T, h2)
    w1_new, h1_new, w2t_new, h2_new = pl.pallas_call(
        finish,
        out_shape=outs,
        in_specs=[vmem] * 4,
        out_specs=(anywhere,) * 4,
        scratch_shapes=[pltpu.SemaphoreType.DMA((4,))],
    )(*[pltpu.with_memory_space_constraint(m, pltpu.VMEM) for m in moved])
    return w1_new, h1_new, w2t_new.T, h2_new


def solution(mesh):
    placed = (P("gene", "cell"), P(("gene", "cell"), None), P(None, "cell"), P(), P(None, "cell"))
    return jax.shard_map(
        on_device,
        mesh=mesh,
        in_specs=placed,
        out_specs=(P(("gene", "cell"), None), P(None, "cell"), P(), P(None, "cell")),
        check_vma=False,
    )
```
